256 devices in a mesh: layer: 64 (over y_hi, z, x), shot: 4 (over y_lo, core).
Axes of the slice: x: 4, y: 4 (y_hi: 2, y_lo: 2; y = y_hi * 2 + y_lo), z: 8, core: 2. Of those that a mesh axis runs over, the one named last changes fastest.
Arguments:
- down_state: bfloat16 [64, 1024, 2048], P('layer', None, 'shot'), may hold values from -6 to 6
- up_state: bfloat16 [64, 1024, 2048], P('layer', None, 'shot'), may hold values from -6 to 6
- down_op: bfloat16 [64, 1024, 1024], P('layer', 'shot'), may hold values from -0.1875 to 0.1875
- up_op: bfloat16 [64, 1024, 1024], P('layer', 'shot'), may hold values from -0.1875 to 0.1875
- reflect_op: bfloat16 [64, 1024, 1024], P('layer', 'shot'), may hold values from -0.125 to 0.125
- source_bank: bfloat16 [64, 2, 1024, 2048], P('layer', None, None, 'shot'), may hold values from -4 to 4
- plan: int32 [4, 64], P(None, 'layer'), may hold values from 0 to 1
- layer_source: int32 [64], P('layer'), may hold values from 0 to 1
Outputs:
- down_out: bfloat16 [64, 1024, 2048], P('layer', None, 'shot')
- up_out: bfloat16 [64, 1024, 2048], P('layer', None, 'shot')
The draws below stay inside these ranges and needn't reach their ends.
All inputs are finite; a program needn't handle non-finite values.
Results may differ from the reference program's by a relative error of at most 0.008.
Values may be sent and summed in bfloat16 or wider, within the bound.
No kernel may reach another device: no remote copies, remote signals or barrier semaphores. Data moves between devices by JAX's collectives and lax.ppermute only.
A program may use at most 64 MiB of HBM per device.

```python
import jax
import jax.numpy as jnp
from jax import lax

M = 1024
NSRC = 2
TICKS = 4
LAYERS = 64
SHOTS = 2048


def touch_ends(result, own_key, smallest, high):
    shape = result.shape
    spot = [jax.random.randint(jax.random.fold_in(own_key, axis), (), 0, shape[axis]) for axis in range(len(shape))]
    result = result.at[tuple(spot)].set(smallest)
    longest = shape.index(max(shape))
    spot[longest] = (spot[longest] + 1) % shape[longest]
    return result.at[tuple(spot)].set(high)


def block_scale(rng, dims, pieces, least, largest):
    def one(axis_at, parts):
        steps = jax.random.uniform(jax.random.fold_in(jax.random.fold_in(rng, 6), axis_at), (parts,), jnp.float32, least / len(pieces), largest / len(pieces))
        return jnp.repeat(jnp.exp(steps), dims[axis_at] // parts).reshape((-1,) + (1,) * (len(dims) - axis_at - 1))

    loudness = one(*pieces[0])
    for cut in pieces[1:]:
        loudness = loudness * one(*cut)
    return loudness


def normal_values(key, extent, width, most, split=(), kind=jnp.bfloat16):
    result = width * jax.random.normal(key, extent, jnp.float32)
    if split:
        result = result * block_scale(key, extent, split, -0.22, 0.18)
    return jnp.clip(result, -most, most).astype(kind)


def setup_inputs(seed: int = 0) -> dict:
    key_of = jax.random.split(jax.random.key(seed), 9)
    return {
        "down_state": normal_values(key_of[0], (LAYERS, M, SHOTS), 1.0, 6.0, ((0, 64), (2, 4))),
        "up_state": normal_values(key_of[1], (LAYERS, M, SHOTS), 1.0, 6.0, ((0, 64), (2, 4))),
        "down_op": normal_values(key_of[2], (LAYERS, M, M), M ** -0.5, 0.1875, ((0, 64), (1, 4))),
        "up_op": normal_values(key_of[3], (LAYERS, M, M), M ** -0.5, 0.1875, ((0, 64), (1, 4))),
        "reflect_op": normal_values(key_of[4], (LAYERS, M, M), (2 * M) ** -0.5, 0.125, ((0, 64), (1, 4))),
        "source_bank": normal_values(key_of[5], (LAYERS, NSRC, M, SHOTS), 0.5, 4.0, ((0, 64), (3, 4))),
        "plan": touch_ends(jax.random.randint(key_of[6], (TICKS, LAYERS), 0, NSRC), jax.random.fold_in(key_of[6], 1), 0, NSRC - 1).astype(jnp.int32),
        "layer_source": touch_ends(jax.random.randint(key_of[7], (LAYERS,), 0, NSRC), jax.random.fold_in(key_of[7], 1), 0, NSRC - 1).astype(jnp.int32),
    }


def layer_update(operands):
    down_block, up_block, reflect_block, down_in, received_up, upward_source = operands
    new_down = jnp.dot(down_block, down_in, preferred_element_type=jnp.float32).astype(jnp.bfloat16)
    total = jnp.dot(up_block, received_up, preferred_element_type=jnp.float32)
    total = total + jnp.dot(reflect_block, down_in, preferred_element_type=jnp.float32)
    total = total + upward_source.astype(jnp.float32)
    return new_down, total.astype(jnp.bfloat16)


def reference(down_state, up_state, down_op, up_op, reflect_op, source_bank, plan, layer_source):
    layer_ids = jnp.arange(LAYERS, dtype=jnp.int32)
    downgoing = down_state
    upgoing = up_state
    upward_source = source_bank[layer_ids, layer_source.astype(jnp.int32)]
    for moment in range(TICKS):
        received_down = jnp.concatenate([jnp.zeros_like(downgoing[:1]), downgoing[:-1]], axis=0)
        received_up = jnp.concatenate([upgoing[1:], jnp.zeros_like(upgoing[:1])], axis=0)
        injected = source_bank[layer_ids, plan[moment].astype(jnp.int32)]
        down_in = (received_down.astype(jnp.float32) + injected.astype(jnp.float32)).astype(jnp.bfloat16)
        downgoing, upgoing = lax.map(layer_update, (down_op, up_op, reflect_op, down_in, received_up, upward_source))
    return downgoing, upgoing
```

```python
import functools

import jax
import jax.numpy as jnp
from jax import lax
from jax.experimental import pallas as pl
from jax.experimental.pallas import tpu as pltpu
from jax.sharding import PartitionSpec as P

TICKS = 4
CHUNKS = 2


def passed_along(value, axis, steps):
    count = lax.axis_size(axis)
    leading, last = (max(0, -steps), min(count, count - steps))
    return lax.ppermute(value, axis, [(source, source + steps) for source in range(leading, last)])


def swapped(value, bit):
    return lax.ppermute(value, "shot", [(i, i ^ bit) for i in range(lax.axis_size("shot"))])


def rows_of(shot, k, height):
    return pl.ds(pl.multiple_of((shot ^ k) * height, height), height)


def down_kernel(info, b0, b1, b2, b3, received, source, *rest):
    new, down_in = rest[-2:]
    shot = info[0]
    down_in[...] = (
        received[...].astype(jnp.float32) + source[...].astype(jnp.float32)
    ).astype(jnp.bfloat16)
    for k, block in enumerate((b0, b1, b2, b3)):
        new[rows_of(shot, k, block.shape[0]), :] = jnp.dot(
            block[...], down_in[...], preferred_element_type=jnp.float32
        ).astype(jnp.bfloat16)


def up_kernel(info, u0, u1, u2, u3, r0, r1, r2, r3, received, down_in, source, *rest):
    new = rest[-1]
    shot = info[0]
    for k, (up, reflect) in enumerate(((u0, r0), (u1, r1), (u2, r2), (u3, r3))):
        rows = rows_of(shot, k, up.shape[0])
        total = jnp.dot(up[...], received[...], preferred_element_type=jnp.float32)
        total = total + jnp.dot(reflect[...], down_in[...], preferred_element_type=jnp.float32)
        total = total + source[rows, :].astype(jnp.float32)
        new[rows, :] = total.astype(jnp.bfloat16)


def state_spec(array, chunk, width):
    height = array.shape[0]
    at = chunk if array.shape[1] > width else 0
    return pl.BlockSpec((height, width), lambda i, info: (0, at))


def call(kernel, name, info, blocks, states, sources, chunk, width, full, n_out, into, flops):
    height, wide = states[0].shape[0], sources.shape[2]
    ops_spec = pl.BlockSpec(blocks[0].shape, lambda i, info: (0, 0))
    in_specs = [ops_spec] * len(blocks)
    in_specs += [state_spec(a, chunk, width) for a in states]
    in_specs += [pl.BlockSpec((None, height, width), lambda i, info: (info[1], 0, chunk))]
    args = [info, *blocks, *states, sources]
    out_shape = [jax.ShapeDtypeStruct((height, wide if full else width), jnp.bfloat16)]
    out_specs = [pl.BlockSpec((height, width), lambda i, info: (0, chunk if full else 0))]
    for _ in range(n_out - 1):
        out_shape.append(jax.ShapeDtypeStruct((height, width), jnp.bfloat16))
        out_specs.append(pl.BlockSpec((height, width), lambda i, info: (0, 0)))
    aliases = {}
    if into is not None:
        in_specs.append(pl.BlockSpec(memory_space=pl.ANY))
        aliases = {len(args): 0}
        args.append(into)
    out = pl.pallas_call(
        kernel,
        name=name,
        out_shape=out_shape,
        grid_spec=pltpu.PrefetchScalarGridSpec(
            num_scalar_prefetch=1, grid=(1,), in_specs=in_specs, out_specs=out_specs
        ),
        input_output_aliases=aliases,
        cost_estimate=pl.CostEstimate(
            flops=flops, transcendentals=0, bytes_accessed=len(blocks) * blocks[0].size * 2
        ),
        compiler_params=pltpu.CompilerParams(vmem_limit_bytes=20 * 2**20),
    )(*args)
    return out


def body(down_state, up_state, down_op, up_op, reflect_op, source_bank, plan, layer_source):
    sources = source_bank[0]
    shot = lax.axis_index("shot").astype(jnp.int32)
    height, wide = down_state.shape[1:]
    width = wide // CHUNKS
    flops = 2 * height * height * width

    downs, ups = [down_state[0]], [up_state[0]]
    far = [swapped(op[0], 2) for op in (down_op, up_op, reflect_op)]
    downs = [passed_along(a, "layer", 1) for a in downs]
    ups = [passed_along(a, "layer", -1) for a in ups]
    near = [swapped(op[0], 1) for op in (down_op, up_op, reflect_op)]
    diagonal = [swapped(a, 1) for a in far]
    blocks = [
        (op[0], near[i], far[i], diagonal[i])
        for i, op in enumerate((down_op, up_op, reflect_op))
    ]
    up_info = jnp.stack([shot, layer_source[0]])
    for moment in range(TICKS):
        last = moment == TICKS - 1
        down_info = jnp.stack([shot, plan[moment, 0]])
        new_downs, new_ups = [], []
        for chunk in range(CHUNKS):
            received_down = downs[chunk if len(downs) > 1 else 0]
            received_up = ups[chunk if len(ups) > 1 else 0]
            new, down_in = call(
                down_kernel, f"down{moment}{chunk}", down_info, blocks[0], [received_down],
                sources, chunk, width, last, 2, new_downs[-1] if last and chunk else None, flops,
            )
            new_downs.append(new)
            (new,) = call(
                up_kernel, f"up{moment}{chunk}", up_info, blocks[1] + blocks[2],
                [received_up, down_in], sources, chunk, width, last, 1,
                new_ups[-1] if last and chunk else None, 2 * flops,
            )
            new_ups.append(new)
        if last:
            return (new_downs[-1][None], new_ups[-1][None])
        downs = [passed_along(a, "layer", 1) for a in new_downs]
        ups = [passed_along(a, "layer", -1) for a in new_ups]


def solution(mesh):
    placed = (
        P("layer", None, "shot"),
        P("layer", None, "shot"),
        P("layer", "shot", None),
        P("layer", "shot", None),
        P("layer", "shot", None),
        P("layer", None, None, "shot"),
        P(None, "layer"),
        P("layer"),
    )
    return jax.shard_map(
        body,
        mesh=mesh,
        in_specs=placed,
        out_specs=(P("layer", None, "shot"), P("layer", None, "shot")),
        check_vma=False,
    )
```

```python
import functools

import jax
import jax.numpy as jnp
from jax import lax
from jax.experimental import pallas as pl
from jax.experimental.pallas import tpu as pltpu
from jax.sharding import PartitionSpec as P


TICKS = 4
CHUNKS = 2
WHOLE = pl.BlockSpec(memory_space=pltpu.VMEM)
SCALARS = pl.BlockSpec(memory_space=pltpu.SMEM)
F32, BF16 = jnp.float32, jnp.bfloat16


def dot(a, b):
    return jnp.dot(a, b, preferred_element_type=F32)


def place():
    spot = lax.axis_index("shot")
    return spot // 2, spot % 2


def band(index, height):
    return pl.ds(pl.multiple_of(index * height, height), height)


def injected(received, source):
    return (received.astype(F32) + source.astype(F32)).astype(BF16)


def first_down_kernel(plan, own, near, received, sources, new, down_in):
    _, core = place()
    down_in[...] = injected(received[...], sources[plan[0, 0]])
    for k, block in enumerate((own, near)):
        new[band(core ^ k, block.shape[0]), :] = dot(block[...], down_in[...]).astype(BF16)


def other_down_kernel(far, diagonal, down_in, new):
    _, core = place()
    for k, block in enumerate((far, diagonal)):
        new[band(core ^ k, block.shape[0]), :] = dot(block[...], down_in[...]).astype(BF16)


def half_up_kernel(half, pick, u0, u1, r0, r1, received, down_in, sources, new):
    side, core = place()
    for k, (up, reflect) in enumerate(((u0, r0), (u1, r1))):
        height = up.shape[0]
        total = dot(up[...], received[...]) + dot(reflect[...], down_in[...])
        rows = band((side ^ half) * 2 + (core ^ k), height)
        total = total + sources[pick[0], rows, :].astype(F32)
        new[band(core ^ k, height), :] = total.astype(BF16)


def stage_kernel(*refs):
    n = (len(refs) - 1) // 2
    copies = [pltpu.make_async_copy(refs[i], refs[n + i], refs[-1].at[i]) for i in range(n)]
    for copy in copies:
        copy.start()
    for copy in copies:
        copy.wait()


def staged(*arrays):
    n = len(arrays)
    return pl.pallas_call(
        stage_kernel,
        name="stage",
        in_specs=[pl.BlockSpec(memory_space=pl.ANY)] * n,
        out_specs=[WHOLE] * n,
        out_shape=[jax.ShapeDtypeStruct(a.shape, a.dtype) for a in arrays],
        scratch_shapes=[pltpu.SemaphoreType.DMA((n,))],
        cost_estimate=pl.CostEstimate(flops=0, transcendentals=0, bytes_accessed=2**20),
        compiler_params=pltpu.CompilerParams(vmem_limit_bytes=16 * 2**20),
    )(*arrays)


def late_kernel(_, down, up, reflect, after, pair):
    high = down.shape[0]
    top = lax.axis_index("layer") == 0
    pair[:high, :] = jnp.where(top, up[...], down[...])
    pair[high:, :] = jnp.where(top, reflect[...], up[...])


def columns(chunk, width):
    return slice(chunk * width, (chunk + 1) * width)


def halves(refs):
    side, _ = place()
    return tuple((band(side ^ k, ref.shape[0]), ref) for k, ref in enumerate(refs))


def down_kernel(moment, chunk, n, last, *refs):
    plan, *blocks = refs[:5]
    received, sources = refs[5 : 5 + n], refs[5 + n]
    late = refs[6 + n : 8 + n] if last else ()
    end = lax.axis_index("layer") == lax.axis_size("layer") - 1
    new, down_in = refs[-2:]
    side, core = place()
    _, width = down_in.shape
    picked, cols = plan[0, moment], columns(chunk, width)
    if n == 1:
        down_in[...] = injected(received[0][...], sources[picked, :, cols])
    else:
        for rows, ref in halves(received):
            down_in[rows, :] = injected(ref[:, cols], sources[picked, rows, cols])
    for k, block in enumerate(blocks):
        high = block.shape[0]
        value = block[...]
        if last and k >= 2:
            value = jnp.where(end, late[k - 2][:high, :], value)
        new[band((side * 2 + core) ^ k, high), :] = dot(value, down_in[...]).astype(BF16)


def up_kernel(chunk, n, last, *refs):
    pick, *blocks = refs[:9]
    received, (down_in, sources) = refs[9 : 9 + n], refs[9 + n : 11 + n]
    late = refs[11 + n : 13 + n] if last else ()
    top = lax.axis_index("layer") == 0
    end = lax.axis_index("layer") == lax.axis_size("layer") - 1
    side, core = place()
    _, width = down_in.shape
    cols = columns(chunk, width)
    if n == 1:
        new, gathered = refs[-1], received[0]
    else:
        new, gathered = refs[-2:]
        for rows, ref in halves(received):
            gathered[rows, :] = ref[:, cols]
    for k in range(4):
        up, reflect = blocks[k][...], blocks[4 + k][...]
        high = up.shape[0]
        if last and k >= 2:
            first, second = late[k - 2][:high, :], late[k - 2][high:, :]
            up = jnp.where(top, first, jnp.where(end, second, up))
            reflect = jnp.where(top, second, reflect)
        rows = band((side * 2 + core) ^ k, high)
        total = dot(up, gathered[...]) + dot(reflect, down_in[...])
        total = total + sources[pick[0], rows, cols].astype(F32)
        new[rows, :] = total.astype(BF16)


def call(kernel, scalars, arrays, out_shape, flops, scratch=(), full=None, into=None, more=()):
    out_specs = [WHOLE] * len(out_shape)
    in_specs = [SCALARS] + [WHOLE] * len(arrays)
    args = [scalars, *arrays]
    in_specs += [WHOLE] * len(more)
    args += more
    aliases = {}
    if full is not None:
        chunk, wide = full
        height, width = out_shape[0]
        out_shape = [(height, wide), *out_shape[1:]]
        out_specs[0] = pl.BlockSpec((height, width), lambda i: (0, chunk))
        if into is not None:
            in_specs.append(pl.BlockSpec(memory_space=pl.ANY))
            aliases = {len(args): 0}
            args.append(into)
            kernel = without(kernel, len(args) - 1)
    return pl.pallas_call(
        kernel,
        grid=(1,),
        in_specs=in_specs,
        out_specs=out_specs,
        out_shape=[jax.ShapeDtypeStruct(s, BF16) for s in out_shape],
        scratch_shapes=list(scratch),
        input_output_aliases=aliases,
        cost_estimate=pl.CostEstimate(flops=flops, transcendentals=0, bytes_accessed=2**20),
        compiler_params=pltpu.CompilerParams(vmem_limit_bytes=16 * 2**20),
    )(*args)


def without(kernel, at):
    def inner(*refs):
        kernel(*refs[:at], *refs[at + 1 :])

    return inner


def sent(value, pairs):
    return lax.ppermute(value, ("layer", "shot"), pairs)


def steps(down_state, up_state, down_op, up_op, reflect_op, source_bank, plan, layer_source):
    layers, shots = lax.axis_size("layer"), lax.axis_size("shot")
    height, wide = down_state.shape[1:]
    width = wide // CHUNKS
    one = 2 * height * height * width
    down_op, up_op, reflect_op = down_op[0], up_op[0], reflect_op[0]

    def at(layer, shot):
        return layer * shots + shot

    every = range(layers)

    def shift(value, steps):
        return sent(value, [
            (at(l, s), at(l + steps, s)) for l in every for s in range(shots) if 0 <= l + steps < layers
        ])

    def swap(value, bit, members):
        return sent(value, [(at(l, s), at(l, s ^ bit)) for l in members for s in range(shots)])

    middle = [l for l in every if 0 < l < layers - 1]
    down_0 = shift(down_state[0], 1)
    far_d = swap(down_op, 2, [0] + middle)
    up_0 = shift(up_state[0], -1)
    near_d = swap(down_op, 1, every)
    far_u = swap(up_op, 2, middle)
    far_r = swap(reflect_op, 2, middle + [layers - 1])
    near_u = swap(up_op, 1, every)
    near_r = swap(reflect_op, 1, every)
    cross_d = swap(far_d, 1, every)
    cross_u = swap(far_u, 1, every)
    cross_r = swap(far_r, 1, every)

    plan = plan.T
    down_op, up_op, reflect_op, sources = staged(down_op, up_op, reflect_op, source_bank[0])
    half = (height // 2, wide)
    new, down_in = call(
        first_down_kernel, plan, [down_op, near_d, down_0, sources],
        [half, (height, wide)], one,
    )
    downs = [shift(new, 1)]
    (new,) = call(
        functools.partial(half_up_kernel, 0), layer_source,
        [up_op, near_u, reflect_op, near_r, up_0, down_in, sources], [half], 2 * one,
    )
    up_near = new
    ups = [shift(new, -1)]
    make = pl.pallas_call(
        other_down_kernel, name="down_far", in_specs=[WHOLE] * 3, out_specs=[WHOLE],
        out_shape=[jax.ShapeDtypeStruct(half, BF16)],
        cost_estimate=pl.CostEstimate(flops=one, transcendentals=0, bytes_accessed=2**20),
        compiler_params=pltpu.CompilerParams(vmem_limit_bytes=16 * 2**20),
    )
    (new,) = make(far_d, cross_d, down_in)
    downs.append(shift(new, 1))
    (new,) = call(
        functools.partial(half_up_kernel, 1), layer_source,
        [far_u, cross_u, far_r, cross_r, up_0, down_in, sources], [half], 2 * one,
    )
    ups.append(shift(new, -1))

    d_blocks = [down_op, near_d, far_d, cross_d]
    u_blocks = [up_op, near_u, far_u, cross_u, reflect_op, near_r, far_r, cross_r]
    late = ()
    for moment in range(1, TICKS):
        last = moment == TICKS - 1
        if moment == 1:
            (pair,) = call(
                late_kernel, layer_source, [down_op, up_op, reflect_op, up_near],
                [(height // 2, height)], one // 8,
            )
            ends = ((0, layers - 4), (layers - 1, 3))
            pair = sent(pair, [(at(a, s), at(b, s)) for a, b in ends for s in range(shots)])
            pair = sent(pair, [(at(b, s), at(a, s ^ 2)) for a, b in ends for s in range(shots)])
            late = (pair, swap(pair, 1, (0, layers - 1)))
        new_downs, new_ups = [], []
        n = len(downs) if moment == 1 else 1
        for chunk in range(CHUNKS):
            full = (chunk, wide) if last else None
            received = downs if moment == 1 else [downs[chunk]]
            new, down_in = call(
                functools.partial(down_kernel, moment, chunk, n, last), plan,
                [*d_blocks, *received, sources], [(height, width)] * 2, one,
                full=full, into=new_downs[-1] if last and chunk else None, more=late if last else (),
            )
            new_downs.append(new)
            received = ups if moment == 1 else [ups[chunk]]
            (new,) = call(
                functools.partial(up_kernel, chunk, n, last), layer_source,
                [*u_blocks, *received, down_in, sources], [(height, width)], 2 * one,
                scratch=[pltpu.VMEM((height, width), BF16)] if n > 1 else [],
                full=full, into=new_ups[-1] if last and chunk else None, more=late if last else (),
            )
            new_ups.append(new)
        if last:
            return (new_downs[-1][None], new_ups[-1][None])
        downs = [shift(a, 1) for a in new_downs]
        ups = [shift(a, -1) for a in new_ups]


def solution(mesh):
    placed = (
        P("layer", None, "shot"),
        P("layer", None, "shot"),
        P("layer", "shot", None),
        P("layer", "shot", None),
        P("layer", "shot", None),
        P("layer", None, None, "shot"),
        P(None, "layer"),
        P("layer"),
    )
    return jax.shard_map(
        steps,
        mesh=mesh,
        in_specs=placed,
        out_specs=(P("layer", None, "shot"), P("layer", None, "shot")),
        check_vma=False,
    )
```

```python
import functools

import jax
import jax.numpy as jnp
from jax import lax
from jax.experimental import pallas as pl
from jax.experimental.pallas import tpu as pltpu
from jax.sharding import PartitionSpec as P


TICKS = 4
CHUNKS = 2
WHOLE = pl.BlockSpec(memory_space=pltpu.VMEM)
SCALARS = pl.BlockSpec(memory_space=pltpu.SMEM)
F32, BF16 = jnp.float32, jnp.bfloat16


def dot(a, b):
    return jnp.dot(a, b, preferred_element_type=F32)


def band(index, height):
    return pl.ds(pl.multiple_of(index * height, height), height)


def injected(received, source):
    return (received.astype(F32) + source.astype(F32)).astype(BF16)


def stage_kernel(*refs):
    n = (len(refs) - 1) // 2
    copies = [pltpu.make_async_copy(refs[i], refs[n + i], refs[-1].at[i]) for i in range(n)]
    for copy in copies:
        copy.start()
    for copy in copies:
        copy.wait()


def staged(*arrays):
    n = len(arrays)
    return pl.pallas_call(
        stage_kernel,
        name="stage",
        in_specs=[pl.BlockSpec(memory_space=pl.ANY)] * n,
        out_specs=[WHOLE] * n,
        out_shape=[jax.ShapeDtypeStruct(a.shape, a.dtype) for a in arrays],
        scratch_shapes=[pltpu.SemaphoreType.DMA((n,))],
        cost_estimate=pl.CostEstimate(flops=0, transcendentals=0, bytes_accessed=2**20),
        compiler_params=pltpu.CompilerParams(vmem_limit_bytes=16 * 2**20),
    )(*arrays)


def late_kernel(_, after, down, up, reflect, pair):
    high = down.shape[0]
    top = lax.axis_index("layer") == 0
    pair[:high, :] = jnp.where(top, up[...], down[...])
    pair[high:, :] = jnp.where(top, reflect[...], up[...])


def columns(ref, chunk, width):
    return slice(chunk * width, (chunk + 1) * width) if ref.shape[-1] > width else slice(None)


def down_kernel(moment, chunk, last, plan, b0, b1, b2, b3, received, sources, *rest):
    late, (new, down_in) = rest[:-2], rest[-2:]
    end = lax.axis_index("layer") == lax.axis_size("layer") - 1
    spot = lax.axis_index("shot")
    width = down_in.shape[1]
    source = sources[plan[0, moment], :, columns(sources, chunk, width)]
    down_in[...] = injected(received[:, columns(received, chunk, width)], source)
    for k, block in enumerate((b0, b1, b2, b3)):
        high, value = block.shape[0], block[...]
        if last and k >= 2:
            value = jnp.where(end, late[k - 2][:high, :], value)
        new[band(spot ^ k, high), :] = dot(value, down_in[...]).astype(BF16)


def up_kernel(chunk, last, *refs):
    pick, *blocks = refs[:9]
    received, down_in, sources = refs[9:12]
    late, new = refs[12:-1], refs[-1]
    top = lax.axis_index("layer") == 0
    end = lax.axis_index("layer") == lax.axis_size("layer") - 1
    spot = lax.axis_index("shot")
    width = down_in.shape[1]
    gathered = received[:, columns(received, chunk, width)]
    for k in range(4):
        up, reflect = blocks[k][...], blocks[4 + k][...]
        high = up.shape[0]
        if last and k >= 2:
            first, second = late[k - 2][:high, :], late[k - 2][high:, :]
            up = jnp.where(top, first, jnp.where(end, second, up))
            reflect = jnp.where(top, second, reflect)
        rows = band(spot ^ k, high)
        total = dot(up, gathered) + dot(reflect, down_in[...])
        total = total + sources[pick[0], rows, columns(sources, chunk, width)].astype(F32)
        new[rows, :] = total.astype(BF16)


def call(kernel, scalars, arrays, out_shape, flops, full=None, into=None, more=()):
    out_specs = [WHOLE] * len(out_shape)
    in_specs = [SCALARS] + [WHOLE] * len(arrays)
    args = [scalars, *arrays]
    in_specs += [WHOLE] * len(more)
    args += more
    aliases = {}
    if full is not None:
        chunk, wide = full
        height, width = out_shape[0]
        out_shape = [(height, wide), *out_shape[1:]]
        out_specs[0] = pl.BlockSpec((height, width), lambda i: (0, chunk))
        if into is not None:
            in_specs.append(pl.BlockSpec(memory_space=pl.ANY))
            aliases = {len(args): 0}
            args.append(into)
            kernel = without(kernel, len(args) - 1)
    return pl.pallas_call(
        kernel,
        grid=(1,),
        in_specs=in_specs,
        out_specs=out_specs,
        out_shape=[jax.ShapeDtypeStruct(s, BF16) for s in out_shape],
        input_output_aliases=aliases,
        cost_estimate=pl.CostEstimate(flops=flops, transcendentals=0, bytes_accessed=2**20),
        compiler_params=pltpu.CompilerParams(vmem_limit_bytes=16 * 2**20),
    )(*args)


def without(kernel, at):
    def inner(*refs):
        kernel(*refs[:at], *refs[at + 1 :])

    return inner


def sent(value, pairs):
    return lax.ppermute(value, ("layer", "shot"), pairs)


def steps(down_state, up_state, down_op, up_op, reflect_op, source_bank, plan, layer_source):
    layers, shots = lax.axis_size("layer"), lax.axis_size("shot")
    height, wide = down_state.shape[1:]
    width = wide // CHUNKS
    one = 2 * height * height * width
    down_op, up_op, reflect_op = down_op[0], up_op[0], reflect_op[0]

    def at(layer, shot):
        return layer * shots + shot

    every = range(layers)

    def shift(value, steps):
        return sent(value, [
            (at(l, s), at(l + steps, s)) for l in every for s in range(shots) if 0 <= l + steps < layers
        ])

    def swap(value, bit, members):
        return sent(value, [(at(l, s), at(l, s ^ bit)) for l in members for s in range(shots)])

    middle = [l for l in every if 0 < l < layers - 1]
    down_0 = shift(down_state[0], 1)
    far_d = swap(down_op, 2, [0] + middle)
    up_0 = shift(up_state[0], -1)
    near_d = swap(down_op, 1, every)
    far_u = swap(up_op, 2, middle)
    far_r = swap(reflect_op, 2, middle + [layers - 1])
    near_u = swap(up_op, 1, every)
    near_r = swap(reflect_op, 1, every)
    cross_d = swap(far_d, 1, every)
    cross_u = swap(far_u, 1, every)
    cross_r = swap(far_r, 1, every)

    plan = plan.T
    down_op, up_op, reflect_op, sources = staged(down_op, up_op, reflect_op, source_bank[0])
    d_blocks = [down_op, near_d, far_d, cross_d]
    u_blocks = [up_op, near_u, far_u, cross_u, reflect_op, near_r, far_r, cross_r]
    downs, ups = [down_0] * CHUNKS, [up_0] * CHUNKS
    late = ()
    for moment in range(TICKS):
        last = moment == TICKS - 1
        if moment == 1:
            (pair,) = call(
                late_kernel, layer_source, [down_in_0, down_op, up_op, reflect_op],
                [(height // 2, height)], one // 8,
            )
            ends = ((0, layers - 4), (layers - 1, 3))
            pair = sent(pair, [(at(a, s), at(b, s)) for a, b in ends for s in range(shots)])
            pair = sent(pair, [(at(b, s), at(a, s ^ 2)) for a, b in ends for s in range(shots)])
            late = (pair, swap(pair, 1, (0, layers - 1)))
        new_downs, new_ups, new, up = [], [], None, None
        for chunk in range(CHUNKS):
            full = (chunk, wide) if last else None
            more = late if last else ()
            new, down_in = call(
                functools.partial(down_kernel, moment, chunk, last), plan,
                [*d_blocks, downs[chunk], sources], [(height, width)] * 2, one,
                full=full, into=new if last else None, more=more,
            )
            (up,) = call(
                functools.partial(up_kernel, chunk, last), layer_source,
                [*u_blocks, ups[chunk], down_in, sources], [(height, width)], 2 * one,
                full=full, into=up if last else None, more=more,
            )
            if moment == 0 and chunk == CHUNKS - 1:
                down_in_0 = down_in
            new_downs.append(new)
            new_ups.append(up)
        if last:
            return (new[None], up[None])
        downs = [shift(a, 1) for a in new_downs]
        ups = [shift(a, -1) for a in new_ups]


def solution(mesh):
    placed = (
        P("layer", None, "shot"),
        P("layer", None, "shot"),
        P("layer", "shot", None),
        P("layer", "shot", None),
        P("layer", "shot", None),
        P("layer", None, None, "shot"),
        P(None, "layer"),
        P("layer"),
    )
    return jax.shard_map(
        steps,
        mesh=mesh,
        in_specs=placed,
        out_specs=(P("layer", None, "shot"), P("layer", None, "shot")),
        check_vma=False,
    )
```

```python
import functools

import jax
import jax.numpy as jnp
from jax import lax
from jax.experimental import pallas as pl
from jax.experimental.pallas import tpu as pltpu
from jax.sharding import PartitionSpec as P


TICKS = 4
CHUNKS = 2
WHOLE = pl.BlockSpec(memory_space=pltpu.VMEM)
SCALARS = pl.BlockSpec(memory_space=pltpu.SMEM)
F32, BF16 = jnp.float32, jnp.bfloat16


def dot(a, b):
    return jnp.dot(a, b, preferred_element_type=F32)


def band(index, height):
    return pl.ds(pl.multiple_of(index * height, height), height)


def injected(received, source):
    return (received.astype(F32) + source.astype(F32)).astype(BF16)


def stage_kernel(*refs):
    n = (len(refs) - 1) // 2
    copies = [pltpu.make_async_copy(refs[i], refs[n + i], refs[-1].at[i]) for i in range(n)]
    for copy in copies:
        copy.start()
    for copy in copies:
        copy.wait()


def staged(*arrays):
    n = len(arrays)
    return pl.pallas_call(
        stage_kernel,
        name="stage",
        in_specs=[pl.BlockSpec(memory_space=pl.ANY)] * n,
        out_specs=[WHOLE] * n,
        out_shape=[jax.ShapeDtypeStruct(a.shape, a.dtype) for a in arrays],
        scratch_shapes=[pltpu.SemaphoreType.DMA((n,))],
        cost_estimate=pl.CostEstimate(flops=0, transcendentals=0, bytes_accessed=2**20),
        compiler_params=pltpu.CompilerParams(vmem_limit_bytes=16 * 2**20),
    )(*arrays)


def late_kernel(_, after, down, up, reflect, first, second):
    top = lax.axis_index("layer") == 0
    first[...] = jnp.where(top, up[...], down[...])
    second[...] = jnp.where(top, reflect[...], up[...])


def near_kernel(plan, own, near, received, sources, new, down_in):
    core = lax.axis_index("shot") % 2
    down_in[...] = injected(received[...], sources[plan[0, 0]])
    for k, block in enumerate((own, near)):
        new[band(core ^ k, block.shape[0]), :] = dot(block[...], down_in[...]).astype(BF16)


def far_kernel(_, far, cross, down_in, *new):
    core = lax.axis_index("shot") % 2
    for k, block in enumerate((far, cross)):
        rows = band(core ^ k, block.shape[0])
        for chunk, ref in enumerate(new):
            cols = columns(down_in, chunk, ref.shape[1])
            ref[rows, :] = dot(block[...], down_in[:, cols]).astype(BF16)


def columns(ref, chunk, width):
    return slice(chunk * width, (chunk + 1) * width) if ref.shape[-1] > width else slice(None)


def down_kernel(moment, chunk, n, last, plan, b0, b1, b2, b3, *rest):
    received, sources, late, (new, down_in) = rest[:n], rest[n], rest[n + 1 : -2], rest[-2:]
    end = lax.axis_index("layer") == lax.axis_size("layer") - 1
    spot = lax.axis_index("shot")
    width = down_in.shape[1]
    cols, picked = columns(sources, chunk, width), plan[0, moment]
    for k, ref in enumerate(received):
        rows = band((spot // 2) ^ k, ref.shape[0]) if n > 1 else slice(None)
        down_in[rows, :] = injected(ref[:, columns(ref, chunk, width)], sources[picked, rows, cols])
    for k, block in enumerate((b0, b1, b2, b3)):
        high, value = block.shape[0], block[...]
        if last and k >= 2:
            value = jnp.where(end, late[k - 2][...], value)
        new[band(spot ^ k, high), :] = dot(value, down_in[...]).astype(BF16)


def up_kernel(chunk, last, *refs):
    pick, *blocks = refs[:9]
    received, down_in, sources = refs[9:12]
    late, new = refs[12:-1], refs[-1]
    top = lax.axis_index("layer") == 0
    end = lax.axis_index("layer") == lax.axis_size("layer") - 1
    spot = lax.axis_index("shot")
    width = new.shape[1]
    gathered = received[:, columns(received, chunk, width)]
    injection = down_in[:, columns(down_in, chunk, width)]
    for k in range(4):
        up, reflect = blocks[k][...], blocks[4 + k][...]
        high = up.shape[0]
        if last and k >= 2:
            first, second = late[k - 2][...], late[k][...]
            up = jnp.where(top, first, jnp.where(end, second, up))
            reflect = jnp.where(top, second, reflect)
        rows = band(spot ^ k, high)
        total = dot(up, gathered) + dot(reflect, injection)
        total = total + sources[pick[0], rows, columns(sources, chunk, width)].astype(F32)
        new[rows, :] = total.astype(BF16)


def call(kernel, scalars, arrays, out_shape, flops, full=None, into=None, more=()):
    out_specs = [WHOLE] * len(out_shape)
    in_specs = [SCALARS] + [WHOLE] * len(arrays)
    args = [scalars, *arrays]
    in_specs += [WHOLE] * len(more)
    args += more
    aliases = {}
    if full is not None:
        chunk, wide = full
        height, width = out_shape[0]
        out_shape = [(height, wide), *out_shape[1:]]
        out_specs[0] = pl.BlockSpec((height, width), lambda i: (0, chunk))
        if into is not None:
            in_specs.append(pl.BlockSpec(memory_space=pl.ANY))
            aliases = {len(args): 0}
            args.append(into)
            kernel = without(kernel, len(args) - 1)
    return pl.pallas_call(
        kernel,
        grid=(1,),
        in_specs=in_specs,
        out_specs=out_specs,
        out_shape=[jax.ShapeDtypeStruct(s, BF16) for s in out_shape],
        input_output_aliases=aliases,
        cost_estimate=pl.CostEstimate(flops=flops, transcendentals=0, bytes_accessed=2**20),
        compiler_params=pltpu.CompilerParams(vmem_limit_bytes=16 * 2**20),
    )(*args)


def without(kernel, at):
    def inner(*refs):
        kernel(*refs[:at], *refs[at + 1 :])

    return inner


def sent(value, pairs):
    return lax.ppermute(value, ("layer", "shot"), pairs)


def steps(down_state, up_state, down_op, up_op, reflect_op, source_bank, plan, layer_source):
    layers, shots = lax.axis_size("layer"), lax.axis_size("shot")
    height, wide = down_state.shape[1:]
    width = wide // CHUNKS
    one = 2 * height * height * width
    down_op, up_op, reflect_op = down_op[0], up_op[0], reflect_op[0]

    def at(layer, shot):
        return layer * shots + shot

    every = range(layers)

    def shift(value, steps, lowest=0):
        return sent(value, [
            (at(l, s), at(l + steps, s)) for l in every for s in range(shots) if lowest <= l + steps < layers
        ])

    def swap(value, bit, members):
        return sent(value, [(at(l, s), at(l, s ^ bit)) for l in members for s in range(shots)])

    middle = [l for l in every if 0 < l < layers - 1]
    down_0 = shift(down_state[0], 1)
    far_d = swap(down_op, 2, [0] + middle)
    up_0 = shift(up_state[0], -1, 1)
    near_d = swap(down_op, 1, every)
    far_u = swap(up_op, 2, middle)
    far_r = swap(reflect_op, 2, middle + [layers - 1])
    near_u = swap(up_op, 1, every)
    near_r = swap(reflect_op, 1, every)
    cross_d = swap(far_d, 1, every)
    cross_u = swap(far_u, 1, every)
    cross_r = swap(far_r, 1, every)

    plan = plan.T
    down_op, up_op, reflect_op, sources = staged(down_op, up_op, reflect_op, source_bank[0])
    d_blocks = [down_op, near_d, far_d, cross_d]
    u_blocks = [up_op, near_u, far_u, cross_u, reflect_op, near_r, far_r, cross_r]
    ends = ((0, layers - 4), (layers - 1, 3))
    out = [(at(a, s), at(b, s)) for a, b in ends for s in range(shots)]
    back = [(at(b, s), at(a, s ^ 2)) for a, b in ends for s in range(shots)]
    half = height // 2
    near, down_in = call(near_kernel, plan, [down_op, near_d, down_0, sources], [(half, wide), (height, wide)], one)
    far = call(far_kernel, layer_source, [far_d, cross_d, down_in], [(half, width)] * CHUNKS, one)
    near = shift(near, 1)
    downs = [[near, shift(a, 1)] for a in far]
    pair = call(
        late_kernel, layer_source, [far[-1], down_op, up_op, reflect_op],
        [down_op.shape] * 2, one // 8,
    )
    late = []
    for a in pair:
        a = sent(sent(a, out), back)
        late += [a, swap(a, 1, (0, layers - 1))]
    ups = [up_0] * CHUNKS
    for moment in range(TICKS):
        last = moment == TICKS - 1
        new_downs, new_ups, new, up = [], [], None, None
        for chunk in range(CHUNKS):
            full = (chunk, wide) if last else None
            if moment:
                new, down_in = call(
                    functools.partial(down_kernel, moment, chunk, len(downs[chunk]), last),
                    plan, [*d_blocks, *downs[chunk], sources],
                    [(height, width)] * 2, one,
                    full=full, into=new if last else None, more=late[:2] if last else (),
                )
                new_downs.append(new)
            (up,) = call(
                functools.partial(up_kernel, chunk, last), layer_source,
                [*u_blocks, ups[chunk], down_in, sources], [(height, width)], 2 * one,
                full=full, into=up if last else None, more=late if last else (),
            )
            new_ups.append(up)
        if last:
            return (new[None], up[None])
        if moment:
            downs = [[shift(a, 1)] for a in new_downs]
        lowest = 0 if moment == TICKS - 2 else 1
        ups = [shift(a, -1, lowest) for a in new_ups]


def solution(mesh):
    placed = (
        P("layer", None, "shot"),
        P("layer", None, "shot"),
        P("layer", "shot", None),
        P("layer", "shot", None),
        P("layer", "shot", None),
        P("layer", None, None, "shot"),
        P(None, "layer"),
        P("layer"),
    )
    return jax.shard_map(
        steps,
        mesh=mesh,
        in_specs=placed,
        out_specs=(P("layer", None, "shot"), P("layer", None, "shot")),
        check_vma=False,
    )
```

```python
import functools

import jax
import jax.numpy as jnp
from jax import lax
from jax.experimental import pallas as pl
from jax.experimental.pallas import tpu as pltpu
from jax.sharding import PartitionSpec as P


TICKS = 4
CHUNKS = 2
WHOLE = pl.BlockSpec(memory_space=pltpu.VMEM)
SCALARS = pl.BlockSpec(memory_space=pltpu.SMEM)
F32, BF16 = jnp.float32, jnp.bfloat16


def dot(a, b):
    return jnp.dot(a, b, preferred_element_type=F32)


def band(index, height):
    return pl.ds(pl.multiple_of(index * height, height), height)


def injected(received, source):
    return (received.astype(F32) + source.astype(F32)).astype(BF16)


def stage_kernel(*refs):
    n = (len(refs) - 1) // 2
    copies = [pltpu.make_async_copy(refs[i], refs[n + i], refs[-1].at[i]) for i in range(n)]
    for copy in copies:
        copy.start()
    for copy in copies:
        copy.wait()


def staged(*arrays):
    n = len(arrays)
    return pl.pallas_call(
        stage_kernel,
        name="stage",
        in_specs=[pl.BlockSpec(memory_space=pl.ANY)] * n,
        out_specs=[WHOLE] * n,
        out_shape=[jax.ShapeDtypeStruct(a.shape, a.dtype) for a in arrays],
        scratch_shapes=[pltpu.SemaphoreType.DMA((n,))],
        cost_estimate=pl.CostEstimate(flops=0, transcendentals=0, bytes_accessed=2**20),
        compiler_params=pltpu.CompilerParams(vmem_limit_bytes=16 * 2**20),
    )(*arrays)


def near_kernel(plan, own, near, received, sources, new):
    core = lax.axis_index("shot") % 2

    @pl.when(lax.axis_index("layer") == 0)
    def _():
        down_in = injected(received[...], sources[plan[0, 0]])
        for k, block in enumerate((own, near)):
            new[band(core ^ k, block.shape[0]), :] = dot(block[...], down_in).astype(BF16)


def far_kernel(_, first, second, new):
    rows = band(1 - lax.axis_index("shot") // 2, new.shape[0])

    @pl.when(lax.axis_index("layer") == 0)
    def _():
        for chunk, ref in enumerate((first, second)):
            new[:, columns(new, chunk, ref.shape[1])] = ref[rows, :]


def products(blocks, down_in, new):
    spot = lax.axis_index("shot")
    for k, block in enumerate(blocks):
        new[band(spot ^ k, block.shape[0]), :] = dot(block[...], down_in[...]).astype(BF16)


def fix_kernel(plan, b0, b1, b2, b3, received, sources, *refs):
    n = len(refs) // 2
    inside = lax.axis_index("layer") == lax.axis_size("layer") // 2

    @pl.when(inside)
    def _():
        for chunk in range(n // 2):
            new, down_in = refs[n + 2 * chunk : n + 2 * chunk + 2]
            cols = columns(sources, chunk, new.shape[1])
            down_in[...] = injected(received[:, cols], sources[plan[0, 0], :, cols])
            products((b0, b1, b2, b3), down_in, new)

    @pl.when(jnp.logical_not(inside))
    def _():
        for old, new in zip(refs[:n], refs[n:]):
            new[...] = old[...]


def columns(ref, chunk, width):
    return slice(chunk * width, (chunk + 1) * width) if ref.shape[-1] > width else slice(None)


def down_kernel(moment, chunk, plan, b0, b1, b2, b3, received, sources, *rest):
    others, (new, down_in) = rest[:-2], rest[-2:]
    layer, count = lax.axis_index("layer"), lax.axis_size("layer")
    spot = lax.axis_index("shot")
    cols = columns(sources, chunk, down_in.shape[1])

    def take(ref, rows=slice(None)):
        value = ref[:, columns(ref, chunk, down_in.shape[1])]
        down_in[rows, :] = injected(value, sources[plan[0, moment], rows, cols])

    if moment == 1:
        near, far, middle = others

        @pl.when(layer == 1)
        def _():
            for k, ref in enumerate((near, far)):
                take(ref, band((spot // 2) ^ k, ref.shape[0]))

        @pl.when(layer == count // 2)
        def _():
            take(middle)

        @pl.when(jnp.logical_and(layer != 1, layer != count // 2))
        def _():
            take(received)

    else:
        take(received)
    for k, block in enumerate((b0, b1, b2, b3)):
        high, value = block.shape[0], block[...]
        if moment == TICKS - 1 and k >= 2:
            value = jnp.where(layer == count - 1, others[k - 2][...], value)
        new[band(spot ^ k, high), :] = dot(value, down_in[...]).astype(BF16)


def up_kernel(chunk, last, *refs):
    pick, *blocks = refs[:9]
    received, down_in, sources = refs[9:12]
    late, new = refs[12:-1], refs[-1]
    top = lax.axis_index("layer") == 0
    end = lax.axis_index("layer") == lax.axis_size("layer") - 1
    spot = lax.axis_index("shot")
    width = new.shape[1]
    gathered = received[:, columns(received, chunk, width)]
    injection = down_in[:, columns(down_in, chunk, width)]
    for k in range(4):
        up, reflect = blocks[k][...], blocks[4 + k][...]
        high = up.shape[0]
        if last and k >= 2:
            up = jnp.where(jnp.logical_or(top, end), late[k - 2][...], up)
            reflect = jnp.where(top, late[k][...], reflect)
        rows = band(spot ^ k, high)
        total = dot(up, gathered) + dot(reflect, injection)
        total = total + sources[pick[0], rows, columns(sources, chunk, width)].astype(F32)
        new[rows, :] = total.astype(BF16)


def call(kernel, scalars, arrays, out_shape, flops, full=None, into=None, more=()):
    out_specs = [WHOLE] * len(out_shape)
    in_specs = [SCALARS] + [WHOLE] * len(arrays)
    args = [scalars, *arrays]
    in_specs += [WHOLE] * len(more)
    args += more
    aliases = {}
    if full is not None:
        chunk, wide = full
        height, width = out_shape[0]
        out_shape = [(height, wide), *out_shape[1:]]
        out_specs[0] = pl.BlockSpec((height, width), lambda i: (0, chunk))
        if into is not None:
            in_specs.append(pl.BlockSpec(memory_space=pl.ANY))
            aliases = {len(args): 0}
            args.append(into)
            kernel = without(kernel, len(args) - 1)
    return pl.pallas_call(
        kernel,
        grid=(1,),
        in_specs=in_specs,
        out_specs=out_specs,
        out_shape=[jax.ShapeDtypeStruct(s, BF16) for s in out_shape],
        input_output_aliases=aliases,
        cost_estimate=pl.CostEstimate(flops=flops, transcendentals=0, bytes_accessed=2**20),
        compiler_params=pltpu.CompilerParams(vmem_limit_bytes=16 * 2**20),
    )(*args)


def without(kernel, at):
    def inner(*refs):
        kernel(*refs[:at], *refs[at + 1 :])

    return inner


def sent(value, pairs):
    return lax.ppermute(value, ("layer", "shot"), pairs)


def steps(down_state, up_state, down_op, up_op, reflect_op, source_bank, plan, layer_source):
    layers, shots = lax.axis_size("layer"), lax.axis_size("shot")
    height, wide = down_state.shape[1:]
    width = wide // CHUNKS
    one = 2 * height * height * width
    down_op, up_op, reflect_op = down_op[0], up_op[0], reflect_op[0]

    def at(layer, shot):
        return layer * shots + shot

    every = range(layers)

    def shift(value, steps, without=()):
        return sent(value, [
            (at(l, s), at(l + steps, s))
            for l in every for s in range(shots) if 0 <= l + steps < layers and l not in without
        ])

    def link(value, pairs, bit):
        return sent(value, [(at(a, s), at(b, s ^ bit)) for a, b in pairs for s in range(shots)])

    def swap(value, bit, members):
        return sent(value, [(at(l, s), at(l, s ^ bit)) for l in members for s in range(shots)])

    middle = [l for l in every if 0 < l < layers - 1]
    cut = layers // 2
    down_0b = link(down_state[0], [(cut - 1, cut)], 0)
    down_0 = shift(down_state[0], 1, [cut - 1])
    far_d = swap(down_op, 2, [0] + middle)
    up_0 = shift(up_state[0], -1, [1])
    far_e = swap(down_op, 2, [layers - 1])
    cross_e = swap(far_e, 1, [layers - 1])
    near_d = swap(down_op, 1, every)
    far_u = swap(up_op, 2, middle)
    far_r = swap(reflect_op, 2, middle + [layers - 1])
    near_u = swap(up_op, 1, every)
    near_r = swap(reflect_op, 1, every)
    cross_d = swap(far_d, 1, every)
    cross_u = swap(far_u, 1, every)
    cross_r = swap(far_r, 1, every)

    plan = plan.T
    down_op, up_op, reflect_op, sources = staged(down_op, up_op, reflect_op, source_bank[0])
    d_blocks = [down_op, near_d, far_d, cross_d]
    u_blocks = [up_op, near_u, far_u, cross_u, reflect_op, near_r, far_r, cross_r]
    ends = ((0, layers - 4), (layers - 1, 3))
    late = []
    for op, pairs in ((up_op, ends), (reflect_op, ends[:1])):
        op = link(op, pairs, 0)
        op = link(op, [(b, a) for a, b in pairs], 2)
        late += [op, link(op, [(a, a) for a, _ in pairs], 1)]
    half = (height // 2, wide)
    piece = (height, width)
    (near,) = call(near_kernel, plan, [down_op, near_d, down_0, sources], [half], one // 8)
    near = link(near, [(0, 1)], 0)
    firsts, middles = [], []
    for chunk in range(CHUNKS):
        new, down_in = call(
            functools.partial(down_kernel, 0, chunk), plan,
            [*d_blocks, down_0, sources], [piece] * 2, one,
        )
        firsts += [new, down_in]
        middles.append(link(new, [(cut - 1, cut)], 0))
    (far,) = call(far_kernel, layer_source, [firsts[0], firsts[2]], [half], one // 8)
    far = link(far, [(0, 1)], 0)
    firsts = call(fix_kernel, plan, [*d_blocks, down_0b, sources, *firsts], [piece] * (2 * CHUNKS), one // 8)
    downs = [shift(firsts[2 * i], 1, [0, cut - 1]) for i in range(CHUNKS)]
    ups = [up_0] * CHUNKS
    for moment in range(TICKS):
        last = moment == TICKS - 1
        new_downs, new_ups, new, up = [], [], None, None
        for chunk in range(CHUNKS):
            full = (chunk, wide) if last else None
            if moment:
                more = [near, far, middles[chunk]] if moment == 1 else [far_e, cross_e] if last else []
                new, down_in = call(
                    functools.partial(down_kernel, moment, chunk), plan,
                    [*d_blocks, downs[chunk], sources], [piece] * 2, one,
                    full=full, into=new if last else None, more=more,
                )
                new_downs.append(new)
            else:
                down_in = firsts[2 * chunk + 1]
            (up,) = call(
                functools.partial(up_kernel, chunk, last), layer_source,
                [*u_blocks, ups[chunk], down_in, sources], [piece], 2 * one,
                full=full, into=up if last else None, more=late if last else (),
            )
            new_ups.append(up)
        if last:
            return (new[None], up[None])
        if moment:
            downs = [shift(a, 1) for a in new_downs]
        without_top = [] if moment == TICKS - 2 else [1]
        ups = [shift(a, -1, without_top) for a in new_ups]


def solution(mesh):
    placed = (
        P("layer", None, "shot"),
        P("layer", None, "shot"),
        P("layer", "shot", None),
        P("layer", "shot", None),
        P("layer", "shot", None),
        P("layer", None, None, "shot"),
        P(None, "layer"),
        P("layer"),
    )
    return jax.shard_map(
        steps,
        mesh=mesh,
        in_specs=placed,
        out_specs=(P("layer", None, "shot"), P("layer", None, "shot")),
        check_vma=False,
    )
```

```python
import functools

import jax
import jax.numpy as jnp
from jax import lax
from jax.experimental import pallas as pl
from jax.experimental.pallas import tpu as pltpu
from jax.sharding import PartitionSpec as P


TICKS = 4
CHUNKS = 2
WHOLE = pl.BlockSpec(memory_space=pltpu.VMEM)
SCALARS = pl.BlockSpec(memory_space=pltpu.SMEM)
F32, BF16 = jnp.float32, jnp.bfloat16


def dot(a, b):
    return jnp.dot(a, b, preferred_element_type=F32)


def band(index, height):
    return pl.ds(pl.multiple_of(index * height, height), height)


def injected(received, source):
    return (received.astype(F32) + source.astype(F32)).astype(BF16)


def stage_kernel(*refs):
    n = (len(refs) - 1) // 2
    copies = [pltpu.make_async_copy(refs[i], refs[n + i], refs[-1].at[i]) for i in range(n)]
    for copy in copies:
        copy.start()
    for copy in copies:
        copy.wait()


def staged(*arrays):
    n = len(arrays)
    return pl.pallas_call(
        stage_kernel,
        name="stage",
        in_specs=[pl.BlockSpec(memory_space=pl.ANY)] * n,
        out_specs=[WHOLE] * n,
        out_shape=[jax.ShapeDtypeStruct(a.shape, a.dtype) for a in arrays],
        scratch_shapes=[pltpu.SemaphoreType.DMA((n,))],
        cost_estimate=pl.CostEstimate(flops=0, transcendentals=0, bytes_accessed=2**20),
        compiler_params=pltpu.CompilerParams(vmem_limit_bytes=16 * 2**20),
    )(*arrays)


def products(blocks, down_in, new):
    spot = lax.axis_index("shot")
    for k, block in enumerate(blocks):
        new[band(spot ^ k, block.shape[0]), :] = dot(block[...], down_in[...]).astype(BF16)


def first_kernel(chunk, plan, b0, b1, b2, b3, received, sources, *rest):
    pair, (new, down_in) = rest[:-2], rest[-2:]
    layer, core = lax.axis_index("layer"), lax.axis_index("shot") % 2
    width = down_in.shape[1]

    def injection(cols):
        return injected(received[:, cols], sources[plan[0, 0], :, cols])

    down_in[...] = injection(columns(sources, chunk, width))

    @pl.when(layer == 0)
    def _():
        for other in range(CHUNKS):
            value = injection(columns(sources, other, width))
            for k, block in enumerate(pair or (b0, b1)):
                high = block.shape[0]
                new[band(other * 2 + (core ^ k), high), :] = dot(block[...], value).astype(BF16)

    @pl.when(layer != 0)
    def _():
        products((b0, b1, b2, b3), down_in, new)


def fix_kernel(plan, b0, b1, b2, b3, received, sources, *refs):
    n = len(refs) // 2
    inside = lax.axis_index("layer") == lax.axis_size("layer") // 2

    @pl.when(inside)
    def _():
        for chunk in range(n // 2):
            new, down_in = refs[n + 2 * chunk : n + 2 * chunk + 2]
            cols = columns(sources, chunk, new.shape[1])
            down_in[...] = injected(received[:, cols], sources[plan[0, 0], :, cols])
            products((b0, b1, b2, b3), down_in, new)

    @pl.when(jnp.logical_not(inside))
    def _():
        for old, new in zip(refs[:n], refs[n:]):
            new[...] = old[...]


def columns(ref, chunk, width):
    return slice(chunk * width, (chunk + 1) * width) if ref.shape[-1] > width else slice(None)


def down_kernel(moment, chunk, plan, b0, b1, b2, b3, received, sources, *rest):
    others, (new, down_in) = rest[:-2], rest[-2:]
    layer, count = lax.axis_index("layer"), lax.axis_size("layer")
    spot = lax.axis_index("shot")
    cols = columns(sources, chunk, down_in.shape[1])

    def take(ref):
        value = ref[:, columns(ref, chunk, down_in.shape[1])]
        down_in[...] = injected(value, sources[plan[0, moment], :, cols])

    if moment == 1:

        @pl.when(layer == 1)
        def _():
            for k, ref in enumerate(others[:2]):
                half = ref.shape[0] // 2
                rows = band((spot // 2) ^ k, half)
                value = ref[chunk * half : (chunk + 1) * half, :]
                down_in[rows, :] = injected(value, sources[plan[0, moment], rows, cols])

        @pl.when(layer == count // 2)
        def _():
            take(others[chunk])

        @pl.when(jnp.logical_and(layer != 1, layer != count // 2))
        def _():
            take(received)

    else:
        take(received)
    for k, block in enumerate((b0, b1, b2, b3)):
        high, value = block.shape[0], block[...]
        if k >= 2:
            value = jnp.where(layer == 0, others[k - 4][...], value)
        if moment == TICKS - 1 and k >= 2:
            value = jnp.where(layer == count - 1, others[k - 2][...], value)
        new[band(spot ^ k, high), :] = dot(value, down_in[...]).astype(BF16)


def up_kernel(chunk, last, *refs):
    pick, *blocks = refs[:9]
    received, down_in, sources = refs[9:12]
    late, new = refs[12:-1], refs[-1]
    top = lax.axis_index("layer") == 0
    end = lax.axis_index("layer") == lax.axis_size("layer") - 1
    spot = lax.axis_index("shot")
    width = new.shape[1]
    gathered = received[:, columns(received, chunk, width)]
    injection = down_in[:, columns(down_in, chunk, width)]
    for k in range(4):
        up, reflect = blocks[k][...], blocks[4 + k][...]
        high = up.shape[0]
        if last and k >= 2:
            up = jnp.where(jnp.logical_or(top, end), late[k - 2][...], up)
            reflect = jnp.where(top, late[k][...], reflect)
        rows = band(spot ^ k, high)
        total = dot(up, gathered) + dot(reflect, injection)
        total = total + sources[pick[0], rows, columns(sources, chunk, width)].astype(F32)
        new[rows, :] = total.astype(BF16)


def call(kernel, scalars, arrays, out_shape, flops, full=None, into=None, more=()):
    out_specs = [WHOLE] * len(out_shape)
    in_specs = [SCALARS] + [WHOLE] * len(arrays)
    args = [scalars, *arrays]
    in_specs += [WHOLE] * len(more)
    args += more
    aliases = {}
    if full is not None:
        chunk, wide = full
        height, width = out_shape[0]
        out_shape = [(height, wide), *out_shape[1:]]
        out_specs[0] = pl.BlockSpec((height, width), lambda i: (0, chunk))
        if into is not None:
            in_specs.append(pl.BlockSpec(memory_space=pl.ANY))
            aliases = {len(args): 0}
            args.append(into)
            kernel = without(kernel, len(args) - 1)
    return pl.pallas_call(
        kernel,
        grid=(1,),
        in_specs=in_specs,
        out_specs=out_specs,
        out_shape=[jax.ShapeDtypeStruct(s, BF16) for s in out_shape],
        input_output_aliases=aliases,
        cost_estimate=pl.CostEstimate(flops=flops, transcendentals=0, bytes_accessed=2**20),
        compiler_params=pltpu.CompilerParams(vmem_limit_bytes=16 * 2**20),
    )(*args)


def without(kernel, at):
    def inner(*refs):
        kernel(*refs[:at], *refs[at + 1 :])

    return inner


def sent(value, pairs):
    return lax.ppermute(value, ("layer", "shot"), pairs)


def steps(down_state, up_state, down_op, up_op, reflect_op, source_bank, plan, layer_source):
    layers, shots = lax.axis_size("layer"), lax.axis_size("shot")
    height, wide = down_state.shape[1:]
    width = wide // CHUNKS
    one = 2 * height * height * width
    down_op, up_op, reflect_op = down_op[0], up_op[0], reflect_op[0]

    def at(layer, shot):
        return layer * shots + shot

    every = range(layers)

    def shift(value, steps, without=()):
        return sent(value, [
            (at(l, s), at(l + steps, s))
            for l in every for s in range(shots) if 0 <= l + steps < layers and l not in without
        ])

    def link(value, pairs, bit):
        return sent(value, [(at(a, s), at(b, s ^ bit)) for a, b in pairs for s in range(shots)])

    def swap(value, bit, members):
        return sent(value, [(at(l, s), at(l, s ^ bit)) for l in members for s in range(shots)])

    middle = [l for l in every if 0 < l < layers - 1]
    cut = layers // 2
    down_0b = link(down_state[0], [(cut - 1, cut)], 0)
    down_0 = shift(down_state[0], 1, [cut - 1])
    far_d = swap(down_op, 2, middle)
    far_0 = swap(down_op, 2, [0])
    cross_0 = swap(far_0, 1, [0])
    up_0 = shift(up_state[0], -1, [1, 2, 3])
    far_e = swap(down_op, 2, [layers - 1])
    cross_e = swap(far_e, 1, [layers - 1])
    near_d = swap(down_op, 1, every)
    far_u = swap(up_op, 2, middle)
    far_r = swap(reflect_op, 2, middle + [layers - 1])
    near_u = swap(up_op, 1, every)
    near_r = swap(reflect_op, 1, every)
    cross_d = swap(far_d, 1, every)
    cross_u = swap(far_u, 1, every)
    cross_r = swap(far_r, 1, every)

    plan = plan.T
    down_op, up_op, reflect_op, sources = staged(down_op, up_op, reflect_op, source_bank[0])
    d_blocks = [down_op, near_d, far_d, cross_d]
    u_blocks = [up_op, near_u, far_u, cross_u, reflect_op, near_r, far_r, cross_r]
    ends = ((0, layers - 4), (layers - 1, 3))
    late = []
    for op, pairs in ((up_op, ends), (reflect_op, ends[:1])):
        op = link(op, pairs, 0)
        op = link(op, [(b, a) for a, b in pairs], 2)
        late += [op, link(op, [(a, a) for a, _ in pairs], 1)]
    piece = (height, width)
    firsts, specials = [], []
    for chunk in range(CHUNKS):
        new, down_in = call(
            functools.partial(first_kernel, chunk), plan,
            [*d_blocks, down_0, sources], [piece] * 2, one, more=[far_0, cross_0] if chunk else [],
        )
        firsts += [new, down_in]
        specials.append(link(new, [(0, 1), (cut - 1, cut)], 0))
    firsts = call(
        fix_kernel, plan, [*d_blocks, down_0b, sources, *firsts], [piece] * (2 * CHUNKS), one // 8
    )
    downs = [shift(firsts[2 * i], 1, [0, cut - 1]) for i in range(CHUNKS)]
    ups = [up_0] * CHUNKS
    for moment in range(TICKS):
        last = moment == TICKS - 1
        new_downs, new_ups, new, up = [], [], None, None
        for chunk in range(CHUNKS):
            full = (chunk, wide) if last else None
            if moment:
                more = specials if moment == 1 else [far_e, cross_e] if last else []
                new, down_in = call(
                    functools.partial(down_kernel, moment, chunk), plan,
                    [*d_blocks, downs[chunk], sources], [piece] * 2, one,
                    full=full, into=new if last else None, more=[*more, far_0, cross_0],
                )
                new_downs.append(new)
            else:
                down_in = firsts[2 * chunk + 1]
            (up,) = call(
                functools.partial(up_kernel, chunk, last), layer_source,
                [*u_blocks, ups[chunk], down_in, sources], [piece], 2 * one,
                full=full, into=up if last else None, more=late if last else (),
            )
            new_ups.append(up)
        if last:
            return (new[None], up[None])
        if moment:
            downs = [shift(a, 1) for a in new_downs]
        without_top = range(1, TICKS - 1 - moment)
        ups = [shift(a, -1, without_top) for a in new_ups]


def solution(mesh):
    placed = (
        P("layer", None, "shot"),
        P("layer", None, "shot"),
        P("layer", "shot", None),
        P("layer", "shot", None),
        P("layer", "shot", None),
        P("layer", None, None, "shot"),
        P(None, "layer"),
        P("layer"),
    )
    return jax.shard_map(
        steps,
        mesh=mesh,
        in_specs=placed,
        out_specs=(P("layer", None, "shot"), P("layer", None, "shot")),
        check_vma=False,
    )
```

```python
import functools

import jax
import jax.numpy as jnp
from jax import lax
from jax.experimental import pallas as pl
from jax.experimental.pallas import tpu as pltpu
from jax.sharding import PartitionSpec as P


TICKS = 4
CHUNKS = 2
WHOLE = pl.BlockSpec(memory_space=pltpu.VMEM)
SCALARS = pl.BlockSpec(memory_space=pltpu.SMEM)
F32, BF16 = jnp.float32, jnp.bfloat16


def dot(a, b):
    return jnp.dot(a, b, preferred_element_type=F32)


def band(index, height):
    return pl.ds(pl.multiple_of(index * height, height), height)


def injected(received, source):
    return (received.astype(F32) + source.astype(F32)).astype(BF16)


def stage_kernel(*refs):
    n = (len(refs) - 1) // 2
    copies = [pltpu.make_async_copy(refs[i], refs[n + i], refs[-1].at[i]) for i in range(n)]
    for copy in copies:
        copy.start()
    for copy in copies:
        copy.wait()


def staged(*arrays):
    n = len(arrays)
    return pl.pallas_call(
        stage_kernel,
        name="stage",
        in_specs=[pl.BlockSpec(memory_space=pltpu.HBM)] * n,
        out_specs=[WHOLE] * n,
        out_shape=[jax.ShapeDtypeStruct(a.shape, a.dtype) for a in arrays],
        scratch_shapes=[pltpu.SemaphoreType.DMA((n,))],
        cost_estimate=pl.CostEstimate(flops=0, transcendentals=0, bytes_accessed=2**20),
        compiler_params=pltpu.CompilerParams(vmem_limit_bytes=16 * 2**20),
    )(*arrays)


def products(blocks, down_in, new):
    spot = lax.axis_index("shot")
    for k, block in enumerate(blocks):
        new[band(spot ^ k, block.shape[0]), :] = dot(block[...], down_in[...]).astype(BF16)


def fix_kernel(plan, b0, b1, b2, b3, received, sources, *refs):
    n = len(refs) // 2
    inside = lax.axis_index("layer") == lax.axis_size("layer") // 2

    @pl.when(inside)
    def _():
        for chunk in range(n // 2):
            new, down_in = refs[n + 2 * chunk : n + 2 * chunk + 2]
            cols = columns(sources, chunk, new.shape[1])
            down_in[...] = injected(received[:, cols], sources[plan[0, 0], :, cols])
            products((b0, b1, b2, b3), down_in, new)

    @pl.when(jnp.logical_not(inside))
    def _():
        for old, new in zip(refs[:n], refs[n:]):
            new[...] = old[...]


def columns(ref, chunk, width):
    return slice(chunk * width, (chunk + 1) * width) if ref.shape[-1] > width else slice(None)


def down_kernel(moment, chunk, plan, b0, b1, b2, b3, received, sources, *rest):
    others, (new, down_in) = rest[:-2], rest[-2:]
    layer, count = lax.axis_index("layer"), lax.axis_size("layer")
    spot = lax.axis_index("shot")
    cols = columns(sources, chunk, down_in.shape[1])

    def take(ref):
        value = ref[:, columns(ref, chunk, down_in.shape[1])]
        down_in[...] = injected(value, sources[plan[0, moment], :, cols])

    if moment == 1:

        @pl.when(layer == count // 2)
        def _():
            take(others[0])

        @pl.when(layer != count // 2)
        def _():
            take(received)

    else:
        take(received)
    for k, block in enumerate((b0, b1, b2, b3)):
        high, value = block.shape[0], block[...]
        if moment == TICKS - 1 and k >= 2:
            value = jnp.where(layer == count - 1, others[k - 2][...], value)
        new[band(spot ^ k, high), :] = dot(value, down_in[...]).astype(BF16)


def up_kernel(chunk, last, *refs):
    pick, *blocks = refs[:9]
    received, down_in, sources = refs[9:12]
    late, new = refs[12:-1], refs[-1]
    top = lax.axis_index("layer") == 0
    end = lax.axis_index("layer") == lax.axis_size("layer") - 1
    spot = lax.axis_index("shot")
    width = new.shape[1]
    gathered = received[:, columns(received, chunk, width)]
    injection = down_in[:, columns(down_in, chunk, width)]
    for k in range(4):
        up, reflect = blocks[k][...], blocks[4 + k][...]
        high = up.shape[0]
        if last and k >= 2:
            up = jnp.where(jnp.logical_or(top, end), late[k - 2][...], up)
            reflect = jnp.where(top, late[k][...], reflect)
        rows = band(spot ^ k, high)
        total = dot(up, gathered) + dot(reflect, injection)
        total = total + sources[pick[0], rows, columns(sources, chunk, width)].astype(F32)
        new[rows, :] = total.astype(BF16)


def call(kernel, scalars, arrays, out_shape, flops, full=None, into=None, more=()):
    out_specs = [WHOLE] * len(out_shape)
    in_specs = [SCALARS] + [WHOLE] * len(arrays)
    args = [scalars, *arrays]
    in_specs += [WHOLE] * len(more)
    args += more
    aliases = {}
    if full is not None:
        chunk, wide = full
        height, width = out_shape[0]
        out_shape = [(height, wide), *out_shape[1:]]
        out_specs[0] = pl.BlockSpec((height, width), lambda i: (0, chunk))
        if into is not None:
            in_specs.append(pl.BlockSpec(memory_space=pl.ANY))
            aliases = {len(args): 0}
            args.append(into)
            kernel = without(kernel, len(args) - 1)
    return pl.pallas_call(
        kernel,
        grid=(1,),
        in_specs=in_specs,
        out_specs=out_specs,
        out_shape=[jax.ShapeDtypeStruct(s, BF16) for s in out_shape],
        input_output_aliases=aliases,
        cost_estimate=pl.CostEstimate(flops=flops, transcendentals=0, bytes_accessed=2**20),
        compiler_params=pltpu.CompilerParams(vmem_limit_bytes=16 * 2**20),
    )(*args)


def without(kernel, at):
    def inner(*refs):
        kernel(*refs[:at], *refs[at + 1 :])

    return inner


def sent(value, pairs):
    return lax.ppermute(value, ("layer", "shot"), pairs)


def steps(down_state, up_state, down_op, up_op, reflect_op, source_bank, plan, layer_source):
    layers, shots = lax.axis_size("layer"), lax.axis_size("shot")
    height, wide = down_state.shape[1:]
    width = wide // CHUNKS
    one = 2 * height * height * width
    down_op, up_op, reflect_op = down_op[0], up_op[0], reflect_op[0]

    def at(layer, shot):
        return layer * shots + shot

    every = range(layers)

    def shift(value, steps, without=()):
        return sent(value, [
            (at(l, s), at(l + steps, s))
            for l in every for s in range(shots) if 0 <= l + steps < layers and l not in without
        ])

    def link(value, pairs, bit):
        return sent(value, [(at(a, s), at(b, s ^ bit)) for a, b in pairs for s in range(shots)])

    def swap(value, bit, members):
        return sent(value, [(at(l, s), at(l, s ^ bit)) for l in members for s in range(shots)])

    middle = [l for l in every if 0 < l < layers - 1]
    cut = layers // 2
    down_0b = link(down_state[0], [(cut - 1, cut)], 0)
    down_0 = shift(down_state[0], 1, [cut - 1])
    far_d = swap(down_op, 2, [0] + middle)
    up_0 = shift(up_state[0], -1, [1, 2, 3])
    far_e = swap(down_op, 2, [layers - 1])
    cross_e = swap(far_e, 1, [layers - 1])
    near_d = swap(down_op, 1, every)
    far_u = swap(up_op, 2, middle)
    far_r = swap(reflect_op, 2, middle + [layers - 1])
    near_u = swap(up_op, 1, every)
    near_r = swap(reflect_op, 1, every)
    cross_d = swap(far_d, 1, every)
    cross_u = swap(far_u, 1, every)
    cross_r = swap(far_r, 1, every)

    plan = plan.T
    down_op, up_op, reflect_op, sources = staged(down_op, up_op, reflect_op, source_bank[0])
    d_blocks = [down_op, near_d, far_d, cross_d]
    u_blocks = [up_op, near_u, far_u, cross_u, reflect_op, near_r, far_r, cross_r]
    ends = ((0, layers - 4), (layers - 1, 3))
    late = []
    for op, pairs in ((up_op, ends), (reflect_op, ends[:1])):
        op = link(op, pairs, 0)
        op = link(op, [(b, a) for a, b in pairs], 2)
        late += [op, link(op, [(a, a) for a, _ in pairs], 1)]
    piece = (height, width)
    firsts, specials = [], []
    for chunk in range(CHUNKS):
        new, down_in = call(
            functools.partial(down_kernel, 0, chunk), plan,
            [*d_blocks, down_0, sources], [piece] * 2, one,
        )
        firsts += [new, down_in]
        specials.append(link(new, [(cut - 1, cut)], 0))
    firsts = call(
        fix_kernel, plan, [*d_blocks, down_0b, sources, *firsts], [piece] * (2 * CHUNKS), one // 8
    )
    downs = [shift(firsts[2 * i], 1, [cut - 1]) for i in range(CHUNKS)]
    ups = [up_0] * CHUNKS
    for moment in range(TICKS):
        last = moment == TICKS - 1
        new_downs, new_ups, new, up = [], [], None, None
        for chunk in range(CHUNKS):
            full = (chunk, wide) if last else None
            if moment:
                more = [specials[chunk]] if moment == 1 else [far_e, cross_e] if last else []
                new, down_in = call(
                    functools.partial(down_kernel, moment, chunk), plan,
                    [*d_blocks, downs[chunk], sources], [piece] * 2, one,
                    full=full, into=new if last else None, more=more,
                )
                new_downs.append(new)
            else:
                down_in = firsts[2 * chunk + 1]
            (up,) = call(
                functools.partial(up_kernel, chunk, last), layer_source,
                [*u_blocks, ups[chunk], down_in, sources], [piece], 2 * one,
                full=full, into=up if last else None, more=late if last else (),
            )
            new_ups.append(up)
        if last:
            return (new[None], up[None])
        if moment:
            downs = [shift(a, 1) for a in new_downs]
        without_top = range(1, TICKS - 1 - moment)
        ups = [shift(a, -1, without_top) for a in new_ups]


def solution(mesh):
    placed = (
        P("layer", None, "shot"),
        P("layer", None, "shot"),
        P("layer", "shot", None),
        P("layer", "shot", None),
        P("layer", "shot", None),
        P("layer", None, None, "shot"),
        P(None, "layer"),
        P("layer"),
    )
    return jax.shard_map(
        steps,
        mesh=mesh,
        in_specs=placed,
        out_specs=(P("layer", None, "shot"), P("layer", None, "shot")),
        check_vma=False,
    )
```

```python
import functools

import jax
import jax.numpy as jnp
from jax import lax
from jax.experimental import pallas as pl
from jax.experimental.pallas import tpu as pltpu
from jax.sharding import PartitionSpec as P


TICKS = 4
CHUNKS = 2
WHOLE = pl.BlockSpec(memory_space=pltpu.VMEM)
SCALARS = pl.BlockSpec(memory_space=pltpu.SMEM)
F32, BF16 = jnp.float32, jnp.bfloat16


def dot(a, b):
    return jnp.dot(a, b, preferred_element_type=F32)


def band(index, height):
    return pl.ds(pl.multiple_of(index * height, height), height)


def injected(received, source):
    return (received.astype(F32) + source.astype(F32)).astype(BF16)


def stage_kernel(*refs):
    n = (len(refs) - 1) // 2
    copies = [pltpu.make_async_copy(refs[i], refs[n + i], refs[-1].at[i]) for i in range(n)]
    for copy in copies:
        copy.start()
    for copy in copies:
        copy.wait()


def staged(*arrays):
    n = len(arrays)
    return pl.pallas_call(
        stage_kernel,
        name="stage",
        in_specs=[pl.BlockSpec(memory_space=pltpu.HBM)] * n,
        out_specs=[WHOLE] * n,
        out_shape=[jax.ShapeDtypeStruct(a.shape, a.dtype) for a in arrays],
        scratch_shapes=[pltpu.SemaphoreType.DMA((n,))],
        cost_estimate=pl.CostEstimate(flops=0, transcendentals=0, bytes_accessed=2**20),
        compiler_params=pltpu.CompilerParams(vmem_limit_bytes=16 * 2**20),
    )(*arrays)


def columns(ref, chunk, width):
    return slice(chunk * width, (chunk + 1) * width) if ref.shape[-1] > width else slice(None)


def down_kernel(moment, chunk, plan, b0, b1, b2, b3, received, sources, *rest):
    others, (new, down_in) = rest[:-2], rest[-2:]
    layer, count = lax.axis_index("layer"), lax.axis_size("layer")
    spot = lax.axis_index("shot")
    cols = columns(sources, chunk, down_in.shape[1])

    source = sources[plan[0, moment], :, cols]
    down_in[...] = injected(received[:, columns(received, chunk, down_in.shape[1])], source)
    for k, block in enumerate((b0, b1, b2, b3)):
        high, value = block.shape[0], block[...]
        if moment == TICKS - 1 and k >= 2:
            value = jnp.where(layer == count - 1, others[k - 2][...], value)
        new[band(spot ^ k, high), :] = dot(value, down_in[...]).astype(BF16)


def up_kernel(chunk, last, *refs):
    pick, *blocks = refs[:9]
    received, down_in, sources = refs[9:12]
    late, new = refs[12:-1], refs[-1]
    top = lax.axis_index("layer") == 0
    end = lax.axis_index("layer") == lax.axis_size("layer") - 1
    spot = lax.axis_index("shot")
    width = new.shape[1]
    gathered = received[:, columns(received, chunk, width)]
    injection = down_in[:, columns(down_in, chunk, width)]
    for k in range(4):
        up, reflect = blocks[k][...], blocks[4 + k][...]
        high = up.shape[0]
        if last and k >= 2:
            up = jnp.where(jnp.logical_or(top, end), late[k - 2][...], up)
            reflect = jnp.where(top, late[k][...], reflect)
        rows = band(spot ^ k, high)
        total = dot(up, gathered) + dot(reflect, injection)
        total = total + sources[pick[0], rows, columns(sources, chunk, width)].astype(F32)
        new[rows, :] = total.astype(BF16)


def call(kernel, scalars, arrays, out_shape, flops, full=None, into=None, more=()):
    out_specs = [WHOLE] * len(out_shape)
    in_specs = [SCALARS] + [WHOLE] * len(arrays)
    args = [scalars, *arrays]
    in_specs += [WHOLE] * len(more)
    args += more
    aliases = {}
    if full is not None:
        chunk, wide = full
        height, width = out_shape[0]
        out_shape = [(height, wide), *out_shape[1:]]
        out_specs[0] = pl.BlockSpec((height, width), lambda i: (0, chunk))
        if into is not None:
            in_specs.append(pl.BlockSpec(memory_space=pl.ANY))
            aliases = {len(args): 0}
            args.append(into)
            kernel = without(kernel, len(args) - 1)
    return pl.pallas_call(
        kernel,
        grid=(1,),
        in_specs=in_specs,
        out_specs=out_specs,
        out_shape=[jax.ShapeDtypeStruct(s, BF16) for s in out_shape],
        input_output_aliases=aliases,
        cost_estimate=pl.CostEstimate(flops=flops, transcendentals=0, bytes_accessed=2**20),
        compiler_params=pltpu.CompilerParams(vmem_limit_bytes=16 * 2**20),
    )(*args)


def without(kernel, at):
    def inner(*refs):
        kernel(*refs[:at], *refs[at + 1 :])

    return inner


def sent(value, pairs):
    return lax.ppermute(value, ("layer", "shot"), pairs)


def steps(down_state, up_state, down_op, up_op, reflect_op, source_bank, plan, layer_source):
    layers, shots = lax.axis_size("layer"), lax.axis_size("shot")
    height, wide = down_state.shape[1:]
    width = wide // CHUNKS
    one = 2 * height * height * width
    down_op, up_op, reflect_op = down_op[0], up_op[0], reflect_op[0]

    def at(layer, shot):
        return layer * shots + shot

    every = range(layers)

    def shift(value, steps, without=()):
        return sent(value, [
            (at(l, s), at(l + steps, s))
            for l in every for s in range(shots) if 0 <= l + steps < layers and l not in without
        ])

    def link(value, pairs, bit):
        return sent(value, [(at(a, s), at(b, s ^ bit)) for a, b in pairs for s in range(shots)])

    def swap(value, bit, members):
        return sent(value, [(at(l, s), at(l, s ^ bit)) for l in members for s in range(shots)])

    middle = [l for l in every if 0 < l < layers - 1]
    down_0 = shift(down_state[0], 1)
    far_d = swap(down_op, 2, [0] + middle)
    up_0 = shift(up_state[0], -1, [1, 2, 3])
    far_e = swap(down_op, 2, [layers - 1])
    cross_e = swap(far_e, 1, [layers - 1])
    near_d = swap(down_op, 1, every)
    far_u = swap(up_op, 2, middle)
    far_r = swap(reflect_op, 2, middle + [layers - 1])
    near_u = swap(up_op, 1, every)
    near_r = swap(reflect_op, 1, every)
    cross_d = swap(far_d, 1, every)
    cross_u = swap(far_u, 1, every)
    cross_r = swap(far_r, 1, every)

    plan = plan.T
    down_op, up_op, reflect_op, sources = staged(down_op, up_op, reflect_op, source_bank[0])
    d_blocks = [down_op, near_d, far_d, cross_d]
    u_blocks = [up_op, near_u, far_u, cross_u, reflect_op, near_r, far_r, cross_r]
    ends = ((0, layers - 4), (layers - 1, 3))
    late = []
    for op, pairs in ((up_op, ends), (reflect_op, ends[:1])):
        op = link(op, pairs, 0)
        op = link(op, [(b, a) for a, b in pairs], 2)
        late += [op, link(op, [(a, a) for a, _ in pairs], 1)]
    piece = (height, width)
    downs, ups = [down_0] * CHUNKS, [up_0] * CHUNKS
    for moment in range(TICKS):
        last = moment == TICKS - 1
        new_downs, new_ups, new, up = [], [], None, None
        for chunk in range(CHUNKS):
            full = (chunk, wide) if last else None
            new, down_in = call(
                functools.partial(down_kernel, moment, chunk), plan,
                [*d_blocks, downs[chunk], sources], [piece] * 2, one,
                full=full, into=new if last else None, more=[far_e, cross_e] if last else [],
            )
            new_downs.append(new)
            (up,) = call(
                functools.partial(up_kernel, chunk, last), layer_source,
                [*u_blocks, ups[chunk], down_in, sources], [piece], 2 * one,
                full=full, into=up if last else None, more=late if last else (),
            )
            new_ups.append(up)
        if last:
            return (new[None], up[None])
        downs = [shift(a, 1) for a in new_downs]
        without_top = range(1, TICKS - 1 - moment)
        ups = [shift(a, -1, without_top) for a in new_ups]


def solution(mesh):
    placed = (
        P("layer", None, "shot"),
        P("layer", None, "shot"),
        P("layer", "shot", None),
        P("layer", "shot", None),
        P("layer", "shot", None),
        P("layer", None, None, "shot"),
        P(None, "layer"),
        P("layer"),
    )
    return jax.shard_map(
        steps,
        mesh=mesh,
        in_specs=placed,
        out_specs=(P("layer", None, "shot"), P("layer", None, "shot")),
        check_vma=False,
    )
```

```python
import functools

import jax
import jax.numpy as jnp
from jax import lax
from jax.experimental import pallas as pl
from jax.experimental.pallas import tpu as pltpu
from jax.sharding import PartitionSpec as P


TICKS = 4
CHUNKS = 2
WHOLE = pl.BlockSpec(memory_space=pltpu.VMEM)
SCALARS = pl.BlockSpec(memory_space=pltpu.SMEM)
F32, BF16 = jnp.float32, jnp.bfloat16


def dot(a, b):
    return jnp.dot(a, b, preferred_element_type=F32)


def band(index, height):
    return pl.ds(pl.multiple_of(index * height, height), height)


def injected(received, source):
    return (received.astype(F32) + source.astype(F32)).astype(BF16)


def stage_kernel(*refs):
    n = (len(refs) - 1) // 2
    copies = [pltpu.make_async_copy(refs[i], refs[n + i], refs[-1].at[i]) for i in range(n)]
    for copy in copies:
        copy.start()
    for copy in copies:
        copy.wait()


def staged(*arrays):
    n = len(arrays)
    return pl.pallas_call(
        stage_kernel,
        name="stage",
        in_specs=[pl.BlockSpec(memory_space=pltpu.HBM)] * n,
        out_specs=[WHOLE] * n,
        out_shape=[jax.ShapeDtypeStruct(a.shape, a.dtype) for a in arrays],
        scratch_shapes=[pltpu.SemaphoreType.DMA((n,))],
        cost_estimate=pl.CostEstimate(flops=0, transcendentals=0, bytes_accessed=2**20),
        compiler_params=pltpu.CompilerParams(vmem_limit_bytes=16 * 2**20),
    )(*arrays)


def columns(ref, chunk, width):
    return slice(chunk * width, (chunk + 1) * width) if ref.shape[-1] > width else slice(None)


class Result:
    def __init__(self, new, space, done, chunk):
        self.new, self.space, self.done, self.copies = new, space, done, []
        self.columns = slice(chunk * space.shape[1], (chunk + 1) * space.shape[1])

    def put(self, k, rows, value):
        self.space[rows, :] = value
        copy = pltpu.make_async_copy(
            self.space.at[rows, :], self.new.at[rows, self.columns], self.done.at[k]
        )
        copy.start()
        self.copies.append(copy)

    def finish(self):
        for copy in self.copies:
            copy.wait()


class Plain:
    def __init__(self, new):
        self.new = new

    def put(self, k, rows, value):
        self.new[rows, :] = value

    def finish(self):
        pass


def down_kernel(moment, chunk, plan, b0, b1, b2, b3, received, sources, *rest):
    if moment == TICKS - 1:
        others, (new, down_in, space, done) = rest[:-4], rest[-4:]
        out = Result(new, space, done, chunk)
    else:
        others, (new, down_in) = rest[:-2], rest[-2:]
        out = Plain(new)
    layer, count = lax.axis_index("layer"), lax.axis_size("layer")
    spot = lax.axis_index("shot")
    cols = columns(sources, chunk, down_in.shape[1])

    source = sources[plan[0, moment], :, cols]
    down_in[...] = injected(received[:, columns(received, chunk, down_in.shape[1])], source)
    for k, block in enumerate((b0, b1, b2, b3)):
        high, value = block.shape[0], block[...]
        if moment == TICKS - 1 and k >= 2:
            value = jnp.where(layer == count - 1, others[k - 2][...], value)
        out.put(k, band(spot ^ k, high), dot(value, down_in[...]).astype(BF16))
    out.finish()


def up_kernel(chunk, last, *refs):
    pick, *blocks = refs[:9]
    received, down_in, sources = refs[9:12]
    if last:
        late, (new, space, done) = refs[12:-3], refs[-3:]
        out, width = Result(new, space, done, chunk), space.shape[1]
    else:
        late, new = (), refs[-1]
        out, width = Plain(new), new.shape[1]
    top = lax.axis_index("layer") == 0
    end = lax.axis_index("layer") == lax.axis_size("layer") - 1
    spot = lax.axis_index("shot")
    gathered = received[:, columns(received, chunk, width)]
    injection = down_in[:, columns(down_in, chunk, width)]
    for k in range(4):
        up, reflect = blocks[k][...], blocks[4 + k][...]
        high = up.shape[0]
        if last and k >= 2:
            up = jnp.where(jnp.logical_or(top, end), late[k - 2][...], up)
            reflect = jnp.where(top, late[k][...], reflect)
        rows = band(spot ^ k, high)
        total = dot(up, gathered) + dot(reflect, injection)
        total = total + sources[pick[0], rows, columns(sources, chunk, width)].astype(F32)
        out.put(k, rows, total.astype(BF16))
    out.finish()


def call(kernel, scalars, arrays, out_shape, flops, full=None, into=None, more=()):
    out_specs = [WHOLE] * len(out_shape)
    in_specs = [SCALARS] + [WHOLE] * len(arrays)
    args = [scalars, *arrays]
    in_specs += [WHOLE] * len(more)
    args += more
    aliases, scratch = {}, []
    if full is not None:
        _, wide = full
        height, width = out_shape[0]
        out_shape = [(height, wide), *out_shape[1:]]
        out_specs[0] = pl.BlockSpec(memory_space=pl.ANY)
        scratch = [pltpu.VMEM((height, width), BF16), pltpu.SemaphoreType.DMA((4,))]
        if into is not None:
            in_specs.append(pl.BlockSpec(memory_space=pl.ANY))
            aliases = {len(args): 0}
            args.append(into)
            kernel = without(kernel, len(args) - 1)
    return pl.pallas_call(
        kernel,
        grid=(1,),
        in_specs=in_specs,
        out_specs=out_specs,
        out_shape=[jax.ShapeDtypeStruct(s, BF16) for s in out_shape],
        scratch_shapes=scratch,
        input_output_aliases=aliases,
        cost_estimate=pl.CostEstimate(flops=flops, transcendentals=0, bytes_accessed=2**20),
        compiler_params=pltpu.CompilerParams(vmem_limit_bytes=16 * 2**20),
    )(*args)


def without(kernel, at):
    def inner(*refs):
        kernel(*refs[:at], *refs[at + 1 :])

    return inner


def sent(value, pairs):
    return lax.ppermute(value, ("layer", "shot"), pairs)


def steps(down_state, up_state, down_op, up_op, reflect_op, source_bank, plan, layer_source):
    layers, shots = lax.axis_size("layer"), lax.axis_size("shot")
    height, wide = down_state.shape[1:]
    width = wide // CHUNKS
    one = 2 * height * height * width
    down_op, up_op, reflect_op = down_op[0], up_op[0], reflect_op[0]

    def at(layer, shot):
        return layer * shots + shot

    every = range(layers)

    def shift(value, steps, without=()):
        return sent(value, [
            (at(l, s), at(l + steps, s))
            for l in every for s in range(shots) if 0 <= l + steps < layers and l not in without
        ])

    def link(value, pairs, bit):
        return sent(value, [(at(a, s), at(b, s ^ bit)) for a, b in pairs for s in range(shots)])

    def swap(value, bit, members):
        return sent(value, [(at(l, s), at(l, s ^ bit)) for l in members for s in range(shots)])

    middle = [l for l in every if 0 < l < layers - 1]
    down_0 = shift(down_state[0], 1)
    far_d = swap(down_op, 2, [0] + middle)
    up_0 = shift(up_state[0], -1, [1, 2, 3])
    far_e = swap(down_op, 2, [layers - 1])
    cross_e = swap(far_e, 1, [layers - 1])
    near_d = swap(down_op, 1, every)
    far_u = swap(up_op, 2, middle)
    far_r = swap(reflect_op, 2, middle + [layers - 1])
    near_u = swap(up_op, 1, every)
    near_r = swap(reflect_op, 1, every)
    cross_d = swap(far_d, 1, every)
    cross_u = swap(far_u, 1, every)
    cross_r = swap(far_r, 1, every)

    plan = plan.T
    down_op, up_op, reflect_op, sources = staged(down_op, up_op, reflect_op, source_bank[0])
    d_blocks = [down_op, near_d, far_d, cross_d]
    u_blocks = [up_op, near_u, far_u, cross_u, reflect_op, near_r, far_r, cross_r]
    ends = ((0, layers - 4), (layers - 1, 3))
    late = []
    for op, pairs in ((up_op, ends), (reflect_op, ends[:1])):
        op = link(op, pairs, 0)
        op = link(op, [(b, a) for a, b in pairs], 2)
        late += [op, link(op, [(a, a) for a, _ in pairs], 1)]
    piece = (height, width)
    downs, ups = [down_0] * CHUNKS, [up_0] * CHUNKS
    for moment in range(TICKS):
        last = moment == TICKS - 1
        new_downs, new_ups, new, up = [], [], None, None
        for chunk in range(CHUNKS):
            full = (chunk, wide) if last else None
            new, down_in = call(
                functools.partial(down_kernel, moment, chunk), plan,
                [*d_blocks, downs[chunk], sources], [piece] * 2, one,
                full=full, into=new if last else None, more=[far_e, cross_e] if last else [],
            )
            new_downs.append(new)
            (up,) = call(
                functools.partial(up_kernel, chunk, last), layer_source,
                [*u_blocks, ups[chunk], down_in, sources], [piece], 2 * one,
                full=full, into=up if last else None, more=late if last else (),
            )
            new_ups.append(up)
        if last:
            return (new[None], up[None])
        downs = [shift(a, 1) for a in new_downs]
        without_top = range(1, TICKS - 1 - moment)
        ups = [shift(a, -1, without_top) for a in new_ups]


def solution(mesh):
    placed = (
        P("layer", None, "shot"),
        P("layer", None, "shot"),
        P("layer", "shot", None),
        P("layer", "shot", None),
        P("layer", "shot", None),
        P("layer", None, None, "shot"),
        P(None, "layer"),
        P("layer"),
    )
    return jax.shard_map(
        steps,
        mesh=mesh,
        in_specs=placed,
        out_specs=(P("layer", None, "shot"), P("layer", None, "shot")),
        check_vma=False,
    )
```

```python
import functools

import jax
import jax.numpy as jnp
from jax import lax
from jax.experimental import pallas as pl
from jax.experimental.pallas import tpu as pltpu
from jax.sharding import PartitionSpec as P


TICKS = 4
CHUNKS = 2
WHOLE = pl.BlockSpec(memory_space=pltpu.VMEM)
SCALARS = pl.BlockSpec(memory_space=pltpu.SMEM)
F32, BF16 = jnp.float32, jnp.bfloat16


def dot(a, b):
    return jnp.dot(a, b, preferred_element_type=F32)


def band(index, height):
    return pl.ds(pl.multiple_of(index * height, height), height)


def injected(received, source):
    return (received.astype(F32) + source.astype(F32)).astype(BF16)


def stage_kernel(*refs):
    n = (len(refs) - 1) // 2
    copies = [pltpu.make_async_copy(refs[i], refs[n + i], refs[-1].at[i]) for i in range(n)]
    for copy in copies:
        copy.start()
    for copy in copies:
        copy.wait()


def staged(*arrays):
    n = len(arrays)
    return pl.pallas_call(
        stage_kernel,
        name="stage",
        in_specs=[pl.BlockSpec(memory_space=pltpu.HBM)] * n,
        out_specs=[WHOLE] * n,
        out_shape=[jax.ShapeDtypeStruct(a.shape, a.dtype) for a in arrays],
        scratch_shapes=[pltpu.SemaphoreType.DMA((n,))],
        cost_estimate=pl.CostEstimate(flops=0, transcendentals=0, bytes_accessed=2**20),
        compiler_params=pltpu.CompilerParams(vmem_limit_bytes=16 * 2**20),
    )(*arrays)


def columns(ref, chunk, width):
    return slice(chunk * width, (chunk + 1) * width) if ref.shape[-1] > width else slice(None)


class Result:
    def __init__(self, new, space, done, chunk):
        self.new, self.space, self.done, self.copies = new, space, done, []
        self.columns = slice(chunk * space.shape[1], (chunk + 1) * space.shape[1])

    def put(self, k, rows, value):
        self.space[rows, :] = value
        self.send(k, rows)

    def send(self, k, rows):
        copy = pltpu.make_async_copy(
            self.space.at[rows, :], self.new.at[rows, self.columns], self.done.at[k]
        )
        copy.start()
        self.copies.append(copy)

    def finish(self):
        for copy in self.copies:
            copy.wait()


class Plain:
    def __init__(self, new):
        self.new = new

    def put(self, k, rows, value):
        self.new[rows, :] = value

    def finish(self):
        pass


def down_kernel(moment, chunk, plan, b0, b1, b2, b3, received, sources, *rest):
    if moment == TICKS - 1:
        others, (new, down_in, space, done) = rest[:-4], rest[-4:]
        out = Result(new, space, done, chunk)
    else:
        others, (new, down_in) = rest[:-2], rest[-2:]
        out = Plain(new)
    layer, count = lax.axis_index("layer"), lax.axis_size("layer")
    spot = lax.axis_index("shot")
    cols = columns(sources, chunk, down_in.shape[1])

    source = sources[plan[0, moment], :, cols]
    down_in[...] = injected(received[:, columns(received, chunk, down_in.shape[1])], source)
    for k, block in enumerate((b0, b1, b2, b3)):
        high, value = block.shape[0], block[...]
        if moment == TICKS - 1 and k >= 2:
            value = jnp.where(layer == count - 1, others[k - 2][...], value)
        out.put(k, band(spot ^ k, high), dot(value, down_in[...]).astype(BF16))
    out.finish()


def up_kernel(chunk, last, *refs):
    pick, *blocks = refs[:9]
    received, down_in, sources = refs[9:12]
    if last:
        late, (new, space, done) = refs[12:-3], refs[-3:]
        out, width = Result(new, space, done, chunk), space.shape[1]
    else:
        late, new = (), refs[-1]
        out, width = Plain(new), new.shape[1]
    top = lax.axis_index("layer") == 0
    end = lax.axis_index("layer") == lax.axis_size("layer") - 1
    spot = lax.axis_index("shot")
    gathered = received[:, columns(received, chunk, width)]
    injection = down_in[:, columns(down_in, chunk, width)]
    for k in range(4):
        rows = band(spot ^ k, blocks[k].shape[0])

        def result(up, reflect, rows=rows):
            total = dot(up, gathered) + dot(reflect, injection)
            total = total + sources[pick[0], rows, columns(sources, chunk, width)].astype(F32)
            return total.astype(BF16)

        if last and k >= 2:
            outer = jnp.logical_or(top, end)

            @pl.when(outer)
            def _(k=k, rows=rows, result=result):
                reflect = jnp.where(top, late[k][...], blocks[4 + k][...])
                space[rows, :] = result(late[k - 2][...], reflect)

            @pl.when(jnp.logical_not(outer))
            def _(k=k, rows=rows, result=result):
                space[rows, :] = result(blocks[k][...], blocks[4 + k][...])

            out.send(k, rows)
        else:
            out.put(k, rows, result(blocks[k][...], blocks[4 + k][...]))
    out.finish()


def call(kernel, scalars, arrays, out_shape, flops, full=None, into=None, more=()):
    out_specs = [WHOLE] * len(out_shape)
    in_specs = [SCALARS] + [WHOLE] * len(arrays)
    args = [scalars, *arrays]
    in_specs += [WHOLE] * len(more)
    args += more
    aliases, scratch = {}, []
    if full is not None:
        _, wide = full
        height, width = out_shape[0]
        out_shape = [(height, wide), *out_shape[1:]]
        out_specs[0] = pl.BlockSpec(memory_space=pl.ANY)
        scratch = [pltpu.VMEM((height, width), BF16), pltpu.SemaphoreType.DMA((4,))]
        if into is not None:
            in_specs.append(pl.BlockSpec(memory_space=pl.ANY))
            aliases = {len(args): 0}
            args.append(into)
            kernel = without(kernel, len(args) - 1)
    return pl.pallas_call(
        kernel,
        grid=(1,),
        in_specs=in_specs,
        out_specs=out_specs,
        out_shape=[jax.ShapeDtypeStruct(s, BF16) for s in out_shape],
        scratch_shapes=scratch,
        input_output_aliases=aliases,
        cost_estimate=pl.CostEstimate(flops=flops, transcendentals=0, bytes_accessed=2**20),
        compiler_params=pltpu.CompilerParams(vmem_limit_bytes=16 * 2**20),
    )(*args)


def without(kernel, at):
    def inner(*refs):
        kernel(*refs[:at], *refs[at + 1 :])

    return inner


def sent(value, pairs):
    return lax.ppermute(value, ("layer", "shot"), pairs)


def steps(down_state, up_state, down_op, up_op, reflect_op, source_bank, plan, layer_source):
    layers, shots = lax.axis_size("layer"), lax.axis_size("shot")
    height, wide = down_state.shape[1:]
    width = wide // CHUNKS
    one = 2 * height * height * width
    down_op, up_op, reflect_op = down_op[0], up_op[0], reflect_op[0]

    def at(layer, shot):
        return layer * shots + shot

    every = range(layers)

    def shift(value, steps, without=()):
        return sent(value, [
            (at(l, s), at(l + steps, s))
            for l in every for s in range(shots) if 0 <= l + steps < layers and l not in without
        ])

    def link(value, pairs, bit):
        return sent(value, [(at(a, s), at(b, s ^ bit)) for a, b in pairs for s in range(shots)])

    def swap(value, bit, members):
        return sent(value, [(at(l, s), at(l, s ^ bit)) for l in members for s in range(shots)])

    middle = [l for l in every if 0 < l < layers - 1]
    down_0 = shift(down_state[0], 1)
    far_d = swap(down_op, 2, [0] + middle)
    up_0 = shift(up_state[0], -1, [1, 2, 3])
    far_e = swap(down_op, 2, [layers - 1])
    cross_e = swap(far_e, 1, [layers - 1])
    near_d = swap(down_op, 1, every)
    far_u = swap(up_op, 2, middle)
    far_r = swap(reflect_op, 2, middle + [layers - 1])
    near_u = swap(up_op, 1, every)
    near_r = swap(reflect_op, 1, every)
    cross_d = swap(far_d, 1, every)
    cross_u = swap(far_u, 1, every)
    cross_r = swap(far_r, 1, every)

    plan = plan.T
    down_op, up_op, reflect_op, sources = staged(down_op, up_op, reflect_op, source_bank[0])
    d_blocks = [down_op, near_d, far_d, cross_d]
    u_blocks = [up_op, near_u, far_u, cross_u, reflect_op, near_r, far_r, cross_r]
    ends = ((0, layers - 4), (layers - 1, 3))
    late = []
    for op, pairs in ((up_op, ends), (reflect_op, ends[:1])):
        op = link(op, pairs, 0)
        op = link(op, [(b, a) for a, b in pairs], 2)
        late += [op, link(op, [(a, a) for a, _ in pairs], 1)]
    piece = (height, width)
    downs, ups = [down_0] * CHUNKS, [up_0] * CHUNKS
    for moment in range(TICKS):
        last = moment == TICKS - 1
        new_downs, new_ups, new, up = [], [], None, None
        for chunk in range(CHUNKS):
            full = (chunk, wide) if last else None
            new, down_in = call(
                functools.partial(down_kernel, moment, chunk), plan,
                [*d_blocks, downs[chunk], sources], [piece] * 2, one,
                full=full, into=new if last else None, more=[far_e, cross_e] if last else [],
            )
            new_downs.append(new)
            (up,) = call(
                functools.partial(up_kernel, chunk, last), layer_source,
                [*u_blocks, ups[chunk], down_in, sources], [piece], 2 * one,
                full=full, into=up if last else None, more=late if last else (),
            )
            new_ups.append(up)
        if last:
            return (new[None], up[None])
        downs = [shift(a, 1) for a in new_downs]
        without_top = range(1, TICKS - 1 - moment)
        ups = [shift(a, -1, without_top) for a in new_ups]


def solution(mesh):
    placed = (
        P("layer", None, "shot"),
        P("layer", None, "shot"),
        P("layer", "shot", None),
        P("layer", "shot", None),
        P("layer", "shot", None),
        P("layer", None, None, "shot"),
        P(None, "layer"),
        P("layer"),
    )
    return jax.shard_map(
        steps,
        mesh=mesh,
        in_specs=placed,
        out_specs=(P("layer", None, "shot"), P("layer", None, "shot")),
        check_vma=False,
    )
```
